256 devices in a mesh: grp: 8 (over y, core), mat: 32 (over z, x).
Axes of the slice: x: 4, y: 4, z: 8, core: 2. Of those that a mesh axis runs over, the one named last changes fastest.
Arguments:
- basis_values: bfloat16 [4096, 256, 512], P(('grp', 'mat')), may hold values from -6 to 6
- weights: float32 [4096, 256], P(('grp', 'mat')), may hold values from 0.004 to 0.04
- density: bfloat16 [768, 5, 128, 128], P('mat'), may hold values from -0.01171875 to 0.01171875
- block_live: int32 [768, 5], P('mat'), may hold values 0 or 1
- batch_blocks: int32 [4096, 4], P(('grp', 'mat')), may hold values from 0 to 767, as said below
- live_functions: int32 [4096], P(('grp', 'mat')), may hold values from 385 to 512
Outputs:
- site_density: float32 [4096, 256], P(('grp', 'mat'))
- hamiltonian: bfloat16 [768, 5, 128, 128], P('mat', None, 'grp')
The draws below stay inside these ranges and needn't reach their ends.
Inputs may be any that keep to these rules, and one draw needn't show every extreme that they name: `batch_blocks`: each row holds 4 increasing blocks within 5 consecutive blocks. The batches of device d are rows d * 16 to d * 16 + 15, counting devices grp first, and all their blocks lie in 32 consecutive block rows, the first of which is used by some batch of the device and the last by another; some batch spans 5 blocks.
All inputs are finite; a program needn't handle non-finite values. No bound on the sum of `block_live` on one device may be relied on, other than what follows from the above.
Results may differ from the reference program's by a relative error of at most 0.0049.
Values may be sent and summed in bfloat16 or wider, within the bound.
A program may use at most 128 MiB of HBM per device.

```python
import math
import jax
import jax.numpy as jnp
from jax import lax

BLK = 128
NBB = 4
PTS = 256
KB_DEV = 24
BAT_DEV = 16
SPAN = 5
REGION = 32
KB = 768
BATCHES = 4096
N_MAT = 32


def layout(key):
    folded = jax.random.fold_in(key, 4242)
    key_first, key_shift, key_skip = jax.random.split(folded, 3)
    devices_count = BATCHES // BAT_DEV
    firsts = jax.random.randint(key_first, (devices_count,), 0, KB - REGION + 1)
    shifts = jax.random.randint(key_shift, (devices_count, BAT_DEV), 0, REGION - SPAN + 1)
    batch_index = jnp.arange(BAT_DEV)[None, :]
    shifts = jnp.where(batch_index == 0, 0, jnp.where(batch_index == 1, REGION - SPAN, shifts))
    skipped = jax.random.randint(key_skip, (devices_count, BAT_DEV), 0, SPAN)
    skipped = jnp.where(batch_index < 2, 1 + skipped % (SPAN - 2), skipped)
    window = firsts[:, None] + shifts
    slot_index = jnp.arange(NBB)
    blocks = window[:, :, None] + slot_index + (slot_index >= skipped[:, :, None]).astype(jnp.int32)
    return blocks.reshape(BATCHES, NBB).astype(jnp.int32)


def draw_batch_blocks(key, part):
    return layout(key)


def with_ends(drawn, rng, least, largest):
    longest = drawn.shape.index(max(drawn.shape))
    spots = []
    for shift in (0, 1):
        where = [jax.random.randint(jax.random.fold_in(rng, axis), (), 0, length) for axis, length in enumerate(drawn.shape)]
        where[longest] = (where[longest] + shift) % drawn.shape[longest]
        spots.append(tuple(where))
    return drawn.at[spots[0]].set(least).at[spots[1]].set(largest)


def block_scale(stream_key, extent, cuts, smallest, high):
    def one(dim, blocks):
        steps = jax.random.uniform(jax.random.fold_in(jax.random.fold_in(stream_key, 6), dim), (blocks,), jnp.float32, smallest / len(cuts), high / len(cuts))
        return jnp.repeat(jnp.exp(steps), extent[dim] // blocks).reshape((-1,) + (1,) * (len(extent) - dim - 1))

    factor_of = one(*cuts[0])
    for cut in cuts[1:]:
        factor_of = factor_of * one(*cut)
    return factor_of


def centred(key, extent, spread, reach, cuts=(), held_as=jnp.bfloat16):
    drawn = spread * jax.random.normal(key, extent, jnp.float32)
    if cuts:
        drawn = drawn * block_scale(key, extent, cuts, -0.22, 0.18)
    return jnp.clip(drawn, -reach, reach).astype(held_as)


def setup_inputs(seed: int = 0) -> dict:
    streams_of = jax.random.split(jax.random.key(seed), 7)
    return {
        "basis_values": centred(streams_of[0], (BATCHES, PTS, NBB * BLK), 1.0, 6.0, ((0, 256),)),
        "weights": jnp.clip(jnp.exp(math.log(0.04) - 2.30258502 * jax.random.uniform(streams_of[1], (BATCHES, PTS), jnp.float32) ** block_scale(streams_of[1], (BATCHES, PTS), ((0, 256),), -0.2, 0.2)), 0.004, 0.04),
        "density": centred(streams_of[2], (KB, SPAN, BLK, BLK), (1.0 / (NBB * BLK)), 0.01171875, ((0, 32),)),
        "block_live": with_ends((jax.random.randint(streams_of[3], (KB, SPAN), 0, 8) < 7).astype(jnp.int32), jax.random.fold_in(streams_of[3], 1), 0, 1),
        "batch_blocks": draw_batch_blocks(jax.random.fold_in(streams_of[6], 71), 0),
        "live_functions": with_ends(jax.random.randint(streams_of[5], (BATCHES,), (NBB - 1) * BLK + 1, NBB * BLK + 1), jax.random.fold_in(streams_of[5], 1), (NBB - 1) * BLK + 1, NBB * BLK).astype(jnp.int32),
    }


def stored_row(block_index):
    return block_index % N_MAT * KB_DEV + block_index // N_MAT

def reference(basis_values, weights, density, block_live, batch_blocks, live_functions):
    masked_density = density * block_live.astype(jnp.bfloat16)[:, :, None, None]
    batch_width = NBB * BLK
    function_index = jnp.arange(batch_width).astype(jnp.int32)
    slot_index = jnp.arange(NBB)
    upper_half = slot_index[:, None] <= slot_index[None, :]
    step_inputs = (basis_values.reshape(BATCHES // 4, 4, PTS, batch_width), weights.reshape(BATCHES // 4, 4, PTS), batch_blocks.reshape(BATCHES // 4, 4, NBB), live_functions.reshape(BATCHES // 4, 4))

    def integrate(ham_total, inputs):
        values, point_weights, blocks, live_count = inputs
        values = jnp.where(function_index[None, None, :] < live_count[:, None, None], values, jnp.zeros_like(values))
        lower_block = jnp.minimum(blocks[:, :, None], blocks[:, None, :])
        upper_block = jnp.maximum(blocks[:, :, None], blocks[:, None, :])
        row_index = stored_row(lower_block).astype(jnp.int32)
        offset = (upper_block - lower_block).astype(jnp.int32)
        gathered_tiles = masked_density[row_index, offset]
        gathered_tiles = jnp.where(upper_half[None, :, :, None, None], gathered_tiles, jnp.swapaxes(gathered_tiles, -1, -2))
        batch_matrix = gathered_tiles.transpose(0, 1, 3, 2, 4).reshape(4, batch_width, batch_width)
        values_wide = values.astype(jnp.float32)
        product_rows = jnp.einsum('brf,bfg->brg', values_wide, batch_matrix.astype(jnp.float32))
        site_values = lax.optimization_barrier(jnp.sum(product_rows * values_wide, axis=-1))
        potential = point_weights * site_values / jnp.sqrt(1.0 + site_values * site_values)
        weighted = (potential[:, :, None] * values_wide).astype(jnp.bfloat16)
        ham_batch = jnp.einsum('brf,brg->bfg', values_wide, weighted.astype(jnp.float32))
        ham_tiles = ham_batch.reshape(4, NBB, BLK, NBB, BLK).transpose(0, 1, 3, 2, 4)
        increment = jnp.where(upper_half[None, :, :, None, None], ham_tiles, jnp.zeros_like(ham_tiles))
        ham_total = ham_total.at[row_index, offset].add(increment)
        return (ham_total, site_values)
    ham_total, site_values = lax.scan(integrate, jnp.zeros((KB, SPAN, BLK, BLK), jnp.float32), step_inputs)
    hamiltonian = (ham_total * block_live.astype(jnp.float32)[:, :, None, None]).astype(jnp.bfloat16)
    return (site_values.reshape(BATCHES, PTS), hamiltonian)
```

```python
import jax
import jax.numpy as jnp
from jax import lax
from jax.experimental import pallas as pl
from jax.experimental.pallas import tpu as pltpu
from jax.sharding import Mesh
from jax.sharding import PartitionSpec as P

AXES = ("y", "c", "z", "x")
MAT = ("z", "x")
GRP = ("y", "c")
NX, NY, NZ, NC = 4, 4, 8, 2
NG = NY * NC
PLANE = NX * NG
BLK = 128
SLICE = BLK // NG
MESH = pl.DeviceIdType.MESH
MIB = 1 << 20
BF16, F32, I32 = jnp.bfloat16, jnp.float32, jnp.int32


def place():
    return tuple(lax.axis_index(a) for a in AXES)


def peer(i, y, c, x):
    return (y + (i // NX) % NY) % NY, (c + i // (NX * NY)) % NC, (x + i % NX) % NX


def slot_of(y, c, x):
    return x * NG + y * NC + c


def greet(y, c, z, x):
    barrier = pltpu.get_barrier_semaphore()

    def signal(i, carry):
        y2, c2, x2 = peer(i, y, c, x)
        pl.semaphore_signal(barrier, inc=1, device_id=(y2, c2, z, x2), device_id_type=MESH)
        return carry

    lax.fori_loop(1, PLANE, signal, 0)
    for step in (1, NZ - 1):
        pl.semaphore_signal(
            barrier, inc=1, device_id=(y, c, (z + step) % NZ, x), device_id_type=MESH
        )
    pl.semaphore_wait(barrier, PLANE + 1)


def remote(src, dst, send_sem, recv_sem, where):
    return pltpu.make_async_remote_copy(
        src_ref=src,
        dst_ref=dst,
        send_sem=send_sem,
        recv_sem=recv_sem,
        device_id=where,
        device_id_type=MESH,
    )


def await_bytes(ref, sem):
    pltpu.make_async_copy(ref, ref, sem).wait()


def fetch_kernel(
    blocks_ref, live_ref, density_ref, region_ref, lanes_ref,
    own, r1, r2, r3, l1, l2, l3, far, send, first, firsts, firsts_s,
    load_sem, first_send, first_recv, table_sem, ring_send, ring_recv, plane_send, plane_recv,
):
    y, c, z, x = place()
    g = y * NC + c
    me = slot_of(y, c, x)
    right, left = (y, c, (z + 1) % NZ, x), (y, c, (z + NZ - 1) % NZ, x)
    load = pltpu.make_async_copy(density_ref.at[:, :, g], own, load_sem)
    load.start()
    first[...] = jnp.broadcast_to(jnp.min(blocks_ref[...], keepdims=True), first.shape)
    greet(y, c, z, x)

    def tell(i, carry):
        y2, c2, x2 = peer(i, y, c, x)
        remote(first, firsts.at[me], first_send, first_recv, (y2, c2, z, x2)).start()
        return carry

    lax.fori_loop(1, PLANE, tell, 0)
    pltpu.make_async_copy(first, firsts.at[me], first_recv).start()
    load.wait()
    rows, span = own.shape[:2]

    def mask(t, carry):
        for o in range(span):
            own[t, o] = own[t, o] * live_ref[t, o].astype(F32).astype(BF16)
        return carry

    lax.fori_loop(0, rows, mask, 0)

    def hop(k, src, dst, where):
        copy = remote(src, dst, ring_send.at[k], ring_recv.at[k], where)
        copy.start()
        return copy

    half = rows // 2
    hop_r1 = hop(0, own, r1, right)
    hop_l1 = hop(1, own, l1, left)
    await_bytes(firsts, first_recv)
    table = pltpu.make_async_copy(firsts, firsts_s, table_sem)
    table.start()
    table.wait()

    def serve(k, source, z_of):
        m = z_of * NX + x

        def wanted(p):
            f = firsts_s[p, 0, 0]
            return lax.shift_right_logical(f + ((m - f) & (NX * NZ - 1)), 5)

        def one(i, carry):
            y2, c2, x2 = peer(i, y, c, x)
            send[k, i] = source[wanted(slot_of(y2, c2, x2))]
            remote(
                send.at[k, i], region_ref.at[z_of, x, g], plane_send.at[k], plane_recv.at[k],
                (y2, c2, z, x2),
            ).start()
            return carry

        lax.fori_loop(1, PLANE, one, 0)
        send[k, 0] = source[wanted(me)]
        pltpu.make_async_copy(send.at[k, 0], region_ref.at[z_of, x, g], plane_recv.at[k]).start()

    serve(0, own, z)
    hop_r1.wait_recv()
    hop_r2 = hop(2, r1, r2, right)
    hop_l1.wait_recv()
    hop_l2 = hop(3, l1, l2, left)
    serve(1, r1, (z + NZ - 1) % NZ)
    serve(2, l1, (z + 1) % NZ)
    hop_r2.wait_recv()
    hop_r3 = hop(4, r2, r3, right)
    hop_l2.wait_recv()
    hop_l3 = hop(5, l2, l3, left)
    serve(3, r2, (z + NZ - 2) % NZ)
    serve(4, l2, (z + 2) % NZ)
    hop_r3.wait_recv()
    hop_rf = hop(6, r3.at[pl.ds(0, half)], far.at[pl.ds(0, half)], right)
    hop_l3.wait_recv()
    hop_lf = hop(7, l3.at[pl.ds(half, half)], far.at[pl.ds(half, half)], left)
    serve(5, r3, (z + NZ - 3) % NZ)
    serve(6, l3, (z + 3) % NZ)
    lane = lax.broadcasted_iota(I32, (8, 128), 1) // SLICE
    for chunk in range(PLANE * SLICE // 128):
        held = firsts[chunk * 8]
        for d in range(1, 8):
            held = jnp.where(lane == d, firsts[chunk * 8 + d], held)
        lanes_ref[:, chunk * 128 : (chunk + 1) * 128] = held
    hop_rf.wait_recv()
    hop_lf.wait_recv()
    serve(7, far, (z + NZ // 2) % NZ)
    for copy in (hop_r1, hop_l1, hop_r2, hop_l2, hop_r3, hop_l3, hop_rf, hop_lf):
        copy.wait_send()
    others = pl.ds(1, PLANE - 1)
    await_bytes(firsts.at[others], first_send)
    for k in range(NZ):
        await_bytes(send.at[k, others], plane_send.at[k])
    for k, off in enumerate((0, NZ - 1, 1, NZ - 2, 2, NZ - 3, 3, NZ // 2)):
        await_bytes(region_ref.at[(z + off) % NZ], plane_recv.at[k])


def fetch(batch_blocks, block_live, density):
    rows, span = density.shape[:2]
    part = (rows, span, SLICE, BLK)
    sem = pltpu.SemaphoreType.DMA
    return pl.pallas_call(
        fetch_kernel,
        name="fetch",
        out_shape=(
            jax.ShapeDtypeStruct((NZ, NX, NG, span, SLICE, BLK), BF16),
            jax.ShapeDtypeStruct((8, PLANE * SLICE), I32),
        ),
        in_specs=[
            pl.BlockSpec(memory_space=pltpu.VMEM),
            pl.BlockSpec(memory_space=pltpu.SMEM),
            pl.BlockSpec(memory_space=pl.ANY),
        ],
        out_specs=(
            pl.BlockSpec(memory_space=pl.ANY),
            pl.BlockSpec(memory_space=pltpu.VMEM),
        ),
        scratch_shapes=[
            *[pltpu.VMEM(part, BF16)] * 8,
            pltpu.VMEM((NZ, PLANE, span, SLICE, BLK), BF16),
            pltpu.VMEM((8, 128), I32),
            pltpu.VMEM((PLANE, 8, 128), I32),
            pltpu.SMEM((PLANE, 8, 128), I32),
            sem, sem, sem, sem, sem((8,)), sem((8,)), sem((NZ,)), sem((NZ,)),
        ],
        compiler_params=pltpu.CompilerParams(
            collective_id=0, has_side_effects=True, vmem_limit_bytes=32 * MIB
        ),
    )(batch_blocks, block_live, density.reshape(rows, span, NG, SLICE, BLK))


def batch_kernel(
    blocks_ref, live_ref, values_ref, weights_ref, region_ref, site_ref, ham_ref, total, upper
):
    b = pl.program_id(0)
    slots = blocks_ref.shape[1]
    width = slots * BLK
    half = width // 2

    @pl.when(b == 0)
    def _():
        upper[...] = jnp.zeros_like(upper)

        @pl.loop(0, total.shape[0])
        def _(m):
            total[m] = jnp.zeros(total.shape[1:], F32)

    starts = [blocks_ref[b, k] for k in range(slots)]
    homes = [s & (NX * NZ - 1) for s in starts]
    for k in range(slots):
        for l in range(k, slots):
            tile = region_ref[homes[k], :, starts[l] - starts[k]].reshape(BLK, BLK)
            upper[k * BLK : (k + 1) * BLK, l * BLK : (l + 1) * BLK] = tile if k == l else tile + tile
    across = values_ref[0].T
    function_index = lax.broadcasted_iota(I32, across.shape, 0)
    across = jnp.where(function_index < live_ref[b], across, jnp.zeros_like(across))
    wide = across.astype(F32)
    top = jnp.dot(upper[:half], across, preferred_element_type=F32)
    low = jnp.dot(upper[half:, half:], across[half:], preferred_element_type=F32)
    site = jnp.sum(top * wide[:half], axis=0, keepdims=True) + jnp.sum(
        low * wide[half:], axis=0, keepdims=True
    )
    site_ref[pl.ds(b, 1)] = site
    potential = weights_ref[pl.ds(b, 1)] * site / jnp.sqrt(1.0 + site * site)
    weighted = (potential * wide).astype(BF16)
    contract = (((1,), (1,)), ((), ()))
    ham_top = lax.dot_general(across[:half], weighted, contract, preferred_element_type=F32)
    ham_low = lax.dot_general(
        across[half:], weighted[half:], contract, preferred_element_type=F32
    )
    for k in range(slots):
        for l in range(k, slots):
            if k < slots // 2:
                tile = ham_top[k * BLK : (k + 1) * BLK, l * BLK : (l + 1) * BLK]
            else:
                i, j = k - slots // 2, l - slots // 2
                tile = ham_low[i * BLK : (i + 1) * BLK, j * BLK : (j + 1) * BLK]
            total[homes[k], starts[l] - starts[k]] += tile

    @pl.when(b == pl.num_programs(0) - 1)
    def _():
        @pl.loop(0, total.shape[0])
        def _(m):
            for o in range(total.shape[1]):
                ham_ref[m, :, o] = total[m, o].astype(BF16).reshape(NG, SLICE, BLK)


def batches(batch_blocks, live_functions, basis_values, weights, region):
    count, points, width = basis_values.shape
    rows = NZ * NX
    span = region.shape[3]
    region = region.reshape(rows, NG, span, SLICE, BLK)
    once = pl.Buffered(1)
    return pl.pallas_call(
        batch_kernel,
        name="batches",
        grid=(count,),
        out_shape=(
            jax.ShapeDtypeStruct((count, points), F32),
            jax.ShapeDtypeStruct(region.shape, BF16),
        ),
        in_specs=[
            pl.BlockSpec(memory_space=pltpu.SMEM),
            pl.BlockSpec(memory_space=pltpu.SMEM),
            pl.BlockSpec((1, points, width), lambda b: (b, 0, 0)),
            pl.BlockSpec((count, points), lambda b: (0, 0), pipeline_mode=once),
            pl.BlockSpec(region.shape, lambda b: (0, 0, 0, 0, 0), pipeline_mode=once),
        ],
        out_specs=(
            pl.BlockSpec((count, points), lambda b: (0, 0), pipeline_mode=once),
            pl.BlockSpec(region.shape, lambda b: (0, 0, 0, 0, 0), pipeline_mode=once),
        ),
        scratch_shapes=[
            pltpu.VMEM((rows, span, BLK, BLK), F32),
            pltpu.VMEM((width, width), BF16),
        ],
        compiler_params=pltpu.CompilerParams(
            dimension_semantics=("arbitrary",), vmem_limit_bytes=40 * MIB
        ),
    )(batch_blocks, live_functions, basis_values, weights, region)


ORDER = (4, 3, -3, 2, -2, 1, -1, 0)
AHEAD = 3


def give_kernel(
    live_ref, lanes_ref, ham_ref, out_ref,
    got, s4, s3r, s3l, s2r, s2l, s1r, s1l, i3r, i3l, i2r, i2l, i1r, i1l, i0r, i0l,
    plane_send, plane_recv, ring_send, ring_recv,
):
    y, c, z, x = place()
    me = slot_of(y, c, x)
    right, left = (y, c, (z + 1) % NZ, x), (y, c, (z + NZ - 1) % NZ, x)
    rows, span = out_ref.shape[:2]
    depth = rows * SLICE
    half = depth // 2
    greet(y, c, z, x)

    def hand(k):
        z_of = (z + ORDER[k] + NZ) % NZ

        def one(i, carry):
            y2, c2, x2 = peer(i, y, c, x)
            remote(
                ham_ref.at[z_of, x2, y2 * NC + c2], got.at[k, me], plane_send.at[k],
                plane_recv.at[k], (y2, c2, z, x2),
            ).start()
            return carry

        lax.fori_loop(1, PLANE, one, 0)
        pltpu.make_async_copy(
            ham_ref.at[z_of, x, y * NC + c], got.at[k, me], plane_recv.at[k]
        ).start()

    lane = lax.broadcasted_iota(I32, lanes_ref.shape, 1) % SLICE
    first = lanes_ref[...]
    row_index = lax.broadcasted_iota(I32, (depth, PLANE * SLICE), 0)

    def partials(k):
        await_bytes(got.at[k], plane_recv.at[k])
        m = ((z + ORDER[k] + NZ) % NZ) * NX + x
        wanted = lax.shift_right_logical(first + ((m - first) & (NX * NZ - 1)), 5)
        key = (wanted * SLICE + lane)[0:1]
        chosen = jnp.where(row_index == key, 1.0, 0.0).astype(BF16)
        for o in range(span):
            block = got[k, :, o].reshape(PLANE * SLICE, BLK)
            yield o, jnp.dot(chosen, block, preferred_element_type=F32)

    def hop(n, src, dst, where):
        copy = remote(src, dst, ring_send.at[n], ring_recv.at[n], where)
        copy.start()
        return copy

    for k in range(AHEAD):
        hand(k)
    hops = []
    for o, part in partials(0):
        s4[o] = part.astype(BF16)
    hops.append(hop(0, s4.at[:, pl.ds(0, half)], i3r, right))
    hops.append(hop(1, s4.at[:, pl.ds(half, half)], i3l, left))
    chain = ((s3r, i3r, i2r), (s3l, i3l, i2l), (s2r, i2r, i1r), (s2l, i2l, i1l),
             (s1r, i1r, i0r), (s1l, i1l, i0l))
    for k, (mine, came, goes) in enumerate(chain, 1):
        if k + AHEAD - 1 < NZ:
            hand(k + AHEAD - 1)
        for o, part in partials(k):
            if o == 0:
                hops[k - 1].wait_recv()
            if k < 3:
                mine[o] = part.astype(BF16)
            if k == 1:
                mine[o, :half] = (part[:half] + came[o].astype(F32)).astype(BF16)
            elif k == 2:
                mine[o, half:] = (part[half:] + came[o].astype(F32)).astype(BF16)
            else:
                mine[o] = (part + came[o].astype(F32)).astype(BF16)
        hops.append(hop(k + 1, mine, goes, right if k % 2 else left))
    for o, part in partials(NZ - 1):
        if o == 0:
            hops[6].wait_recv()
            hops[7].wait_recv()
        total = part + i0r[o].astype(F32) + i0l[o].astype(F32)
        for t in range(rows):
            live = live_ref[t, o].astype(F32)
            out_ref[t, o] = (total[t * SLICE : (t + 1) * SLICE] * live).astype(BF16)
    for copy in hops:
        copy.wait_send()
    others = pl.ds(1, PLANE - 1)
    for k in range(NZ):
        await_bytes(got.at[k, others], plane_send.at[k])


def give(block_live, lanes, ham, rows):
    span = ham.shape[2]
    sem = pltpu.SemaphoreType.DMA
    whole = pltpu.VMEM((span, rows * SLICE, BLK), BF16)
    part = pltpu.VMEM((span, rows * SLICE // 2, BLK), BF16)
    return pl.pallas_call(
        give_kernel,
        name="give",
        out_shape=jax.ShapeDtypeStruct((rows, span, SLICE, BLK), BF16),
        in_specs=[
            pl.BlockSpec(memory_space=pltpu.SMEM),
            pl.BlockSpec(memory_space=pltpu.VMEM),
            pl.BlockSpec(memory_space=pl.ANY),
        ],
        out_specs=pl.BlockSpec(memory_space=pltpu.VMEM),
        scratch_shapes=[
            pltpu.VMEM((NZ, PLANE, span, SLICE, BLK), BF16),
            *[whole] * 7,
            part, part, *[whole] * 6,
            sem((NZ,)), sem((NZ,)), sem((8,)), sem((8,)),
        ],
        compiler_params=pltpu.CompilerParams(
            collective_id=1, has_side_effects=True, vmem_limit_bytes=40 * MIB
        ),
    )(block_live, lanes, ham.reshape(NZ, NX, NG, span, SLICE, BLK))


def per_device(basis_values, weights, density, block_live, batch_blocks, live_functions):
    region, lanes = fetch(batch_blocks, block_live, density)
    site_density, ham = batches(batch_blocks, live_functions, basis_values, weights, region)
    return site_density, give(block_live, lanes, ham, density.shape[0])


def solution(mesh):
    split = Mesh(mesh.devices.reshape(NY, NC, NZ, NX), AXES)
    placed = (
        P(AXES, None, None),
        P(AXES, None),
        P(MAT, None, None, None),
        P(MAT, None),
        P(AXES, None),
        P(AXES),
    )
    return jax.shard_map(
        per_device,
        mesh=split,
        in_specs=placed,
        out_specs=(P(AXES, None), P(MAT, None, GRP, None)),
        check_vma=False,
    )
```

```python
import jax
import jax.numpy as jnp
from jax import lax
from jax.experimental import pallas as pl
from jax.experimental.pallas import tpu as pltpu
from jax.sharding import Mesh
from jax.sharding import PartitionSpec as P

AXES = ("y", "c", "z", "x")
MAT = ("z", "x")
GRP = ("y", "c")
NX, NY, NZ, NC = 4, 4, 8, 2
NG = NY * NC
PLANE = NX * NG
BLK = 128
SLICE = BLK // NG
MESH = pl.DeviceIdType.MESH
MIB = 1 << 20
BF16, F32, I32 = jnp.bfloat16, jnp.float32, jnp.int32


def place():
    return tuple(lax.axis_index(a) for a in AXES)


def peer(i, y, c, x):
    return (y + (i // NX) % NY) % NY, (c + i // (NX * NY)) % NC, (x + i % NX) % NX


def slot_of(y, c, x):
    return x * NG + y * NC + c


def greet(y, c, z, x):
    barrier = pltpu.get_barrier_semaphore()

    def signal(i, carry):
        y2, c2, x2 = peer(i, y, c, x)
        pl.semaphore_signal(barrier, inc=1, device_id=(y2, c2, z, x2), device_id_type=MESH)
        return carry

    lax.fori_loop(1, PLANE, signal, 0)
    for step in (1, NZ - 1):
        pl.semaphore_signal(
            barrier, inc=1, device_id=(y, c, (z + step) % NZ, x), device_id_type=MESH
        )
    pl.semaphore_wait(barrier, PLANE + 1)


def remote(src, dst, send_sem, recv_sem, where):
    return pltpu.make_async_remote_copy(
        src_ref=src,
        dst_ref=dst,
        send_sem=send_sem,
        recv_sem=recv_sem,
        device_id=where,
        device_id_type=MESH,
    )


def await_bytes(ref, sem):
    pltpu.make_async_copy(ref, ref, sem).wait()


def fetch_kernel(
    blocks_hbm, live_hbm, functions_hbm, density_ref, values_ref,
    region_ref, lanes_ref, across_ref, total_ref,
    own, r1, r2, r3, l1, l2, l3, far, send, first, firsts, firsts_s, blocks_ref, live_ref,
    functions_ref, raw,
    load_sem, first_send, first_recv, table_sem, small_sem, value_sem, ring_send, ring_recv,
    plane_send, plane_recv,
):
    y, c, z, x = place()
    g = y * NC + c
    me = slot_of(y, c, x)
    right, left = (y, c, (z + 1) % NZ, x), (y, c, (z + NZ - 1) % NZ, x)
    small = [
        pltpu.make_async_copy(blocks_hbm, blocks_ref, small_sem.at[0]),
        pltpu.make_async_copy(live_hbm, live_ref, small_sem.at[1]),
        pltpu.make_async_copy(functions_hbm, functions_ref, small_sem.at[2]),
    ]
    for copy in small:
        copy.start()
    load = pltpu.make_async_copy(density_ref.at[:, :, g], own, load_sem)
    load.start()
    greet(y, c, z, x)
    small[0].wait()
    first[...] = jnp.broadcast_to(jnp.min(blocks_ref[...], keepdims=True), first.shape)

    def tell(i, carry):
        y2, c2, x2 = peer(i, y, c, x)
        remote(first, firsts.at[me], first_send, first_recv, (y2, c2, z, x2)).start()
        return carry

    lax.fori_loop(1, PLANE, tell, 0)
    pltpu.make_async_copy(first, firsts.at[me], first_recv).start()
    small[1].wait()
    small[2].wait()
    load.wait()
    rows, span = own.shape[:2]

    def mask(t, carry):
        for o in range(span):
            scale = live_ref[t, o].astype(F32) * (2.0 if o else 1.0)
            own[t, o] = own[t, o] * scale.astype(BF16)
        return carry

    lax.fori_loop(0, rows, mask, 0)

    def hop(k, src, dst, where):
        copy = remote(src, dst, ring_send.at[k], ring_recv.at[k], where)
        copy.start()
        return copy

    half = rows // 2
    hop_r1 = hop(0, own, r1, right)
    hop_l1 = hop(1, own, l1, left)
    count = values_ref.shape[0]
    per = count // NZ

    def bring(b):
        slot = b % (2 * per)
        return pltpu.make_async_copy(values_ref.at[b], raw.at[slot], value_sem.at[slot])

    for b in range(per):
        bring(b).start()
    await_bytes(firsts, first_recv)
    table = pltpu.make_async_copy(firsts, firsts_s, table_sem)
    table.start()
    table.wait()

    def serve(k, source, z_of):
        m = z_of * NX + x

        def wanted(p):
            f = firsts_s[p, 0, 0]
            return lax.shift_right_logical(f + ((m - f) & (NX * NZ - 1)), 5)

        def one(i, carry):
            y2, c2, x2 = peer(i, y, c, x)
            send[k, i] = source[wanted(slot_of(y2, c2, x2))]
            remote(
                send.at[k, i], region_ref.at[z_of, x, g], plane_send.at[k], plane_recv.at[k],
                (y2, c2, z, x2),
            ).start()
            return carry

        lax.fori_loop(1, PLANE, one, 0)
        send[k, 0] = source[wanted(me)]
        pltpu.make_async_copy(send.at[k, 0], region_ref.at[z_of, x, g], plane_recv.at[k]).start()

    def prepare(k):
        for b in range(k * per, (k + 1) * per):
            if b + per < count:
                bring(b + per).start()
        for b in range(k * per, (k + 1) * per):
            bring(b).wait()
            across = raw[b % (2 * per)].T
            function_index = lax.broadcasted_iota(I32, across.shape, 0)
            across_ref[b] = jnp.where(
                function_index < functions_ref[b], across, jnp.zeros_like(across)
            )
        step = total_ref.shape[0] // NZ

        @pl.loop(k * step, (k + 1) * step)
        def _(m):
            total_ref[m] = jnp.zeros(total_ref.shape[1:], F32)

    serve(0, own, z)
    prepare(0)
    hop_r1.wait_recv()
    hop_r2 = hop(2, r1, r2, right)
    hop_l1.wait_recv()
    hop_l2 = hop(3, l1, l2, left)
    serve(1, r1, (z + NZ - 1) % NZ)
    serve(2, l1, (z + 1) % NZ)
    prepare(1)
    prepare(2)
    hop_r2.wait_recv()
    hop_r3 = hop(4, r2, r3, right)
    hop_l2.wait_recv()
    hop_l3 = hop(5, l2, l3, left)
    serve(3, r2, (z + NZ - 2) % NZ)
    serve(4, l2, (z + 2) % NZ)
    prepare(3)
    prepare(4)
    hop_r3.wait_recv()
    hop_rf = hop(6, r3.at[pl.ds(0, half)], far.at[pl.ds(0, half)], right)
    hop_l3.wait_recv()
    hop_lf = hop(7, l3.at[pl.ds(half, half)], far.at[pl.ds(half, half)], left)
    serve(5, r3, (z + NZ - 3) % NZ)
    serve(6, l3, (z + 3) % NZ)
    prepare(5)
    prepare(6)
    hop_rf.wait_recv()
    hop_lf.wait_recv()
    serve(7, far, (z + NZ // 2) % NZ)
    prepare(7)
    lane = lax.broadcasted_iota(I32, (8, 128), 1) // SLICE
    for chunk in range(PLANE * SLICE // 128):
        held = firsts[chunk * 8]
        for d in range(1, 8):
            held = jnp.where(lane == d, firsts[chunk * 8 + d], held)
        lanes_ref[:, chunk * 128 : (chunk + 1) * 128] = held
    for copy in (hop_r1, hop_l1, hop_r2, hop_l2, hop_r3, hop_l3, hop_rf, hop_lf):
        copy.wait_send()
    others = pl.ds(1, PLANE - 1)
    await_bytes(firsts.at[others], first_send)
    for k in range(NZ):
        await_bytes(send.at[k, others], plane_send.at[k])
    for k, off in enumerate((0, NZ - 1, 1, NZ - 2, 2, NZ - 3, 3, NZ // 2)):
        await_bytes(region_ref.at[(z + off) % NZ], plane_recv.at[k])


def fetch(batch_blocks, block_live, live_functions, density, basis_values):
    rows, span = density.shape[:2]
    count, points, width = basis_values.shape
    part = (rows, span, SLICE, BLK)
    sem = pltpu.SemaphoreType.DMA
    far_away = pl.BlockSpec(memory_space=pltpu.HBM)
    near = pl.BlockSpec(memory_space=pltpu.VMEM)
    return pl.pallas_call(
        fetch_kernel,
        name="fetch",
        out_shape=(
            jax.ShapeDtypeStruct((NZ, NX, NG, span, SLICE, BLK), BF16),
            jax.ShapeDtypeStruct((8, PLANE * SLICE), I32),
            jax.ShapeDtypeStruct((count, width, points), BF16),
            jax.ShapeDtypeStruct((NZ * NX, span, BLK, BLK), F32),
        ),
        in_specs=[far_away] * 5,
        out_specs=(near,) * 4,
        scratch_shapes=[
            *[pltpu.VMEM(part, BF16)] * 8,
            pltpu.VMEM((NZ, PLANE, span, SLICE, BLK), BF16),
            pltpu.VMEM((8, 128), I32),
            pltpu.VMEM((PLANE, 8, 128), I32),
            pltpu.SMEM((PLANE, 8, 128), I32),
            pltpu.VMEM(batch_blocks.shape, I32),
            pltpu.SMEM(block_live.shape, I32),
            pltpu.SMEM(live_functions.shape, I32),
            pltpu.VMEM((2 * count // NZ, points, width), BF16),
            sem, sem, sem, sem, sem((3,)), sem((2 * count // NZ,)), sem((8,)), sem((8,)),
            sem((NZ,)), sem((NZ,)),
        ],
        compiler_params=pltpu.CompilerParams(
            collective_id=0, has_side_effects=True, vmem_limit_bytes=16 * MIB
        ),
    )(
        batch_blocks, block_live, live_functions,
        pltpu.with_memory_space_constraint(density.reshape(rows, span, NG, SLICE, BLK), pltpu.HBM),
        pltpu.with_memory_space_constraint(basis_values, pltpu.HBM),
    )


def batch_kernel(blocks_ref, across_ref, weights_ref, region_ref, zeros_ref, site_ref, total):
    del zeros_ref
    count, slots = blocks_ref.shape
    half = slots * BLK // 2
    contract = (((1,), (1,)), ((), ()))

    def one(b, carry):
        starts = [blocks_ref[b, k] for k in range(slots)]
        homes = [s & (NX * NZ - 1) for s in starts]
        across = across_ref[b]

        def tile(k, l):
            return region_ref[homes[k], :, starts[l] - starts[k]].reshape(BLK, BLK)

        wide = across.astype(F32)
        site = jnp.zeros((1, across.shape[1]), F32)
        for k in range(slots):
            tiles = jnp.concatenate([tile(k, l) for l in range(k, slots)], axis=1)
            product = jnp.dot(tiles, across[k * BLK :], preferred_element_type=F32)
            site += jnp.sum(product * wide[k * BLK : (k + 1) * BLK], axis=0, keepdims=True)
        site_ref[pl.ds(b, 1)] = site
        potential = weights_ref[pl.ds(b, 1)] * site / jnp.sqrt(1.0 + site * site)
        weighted = (potential * wide).astype(BF16)
        top = lax.dot_general(across[:half], weighted, contract, preferred_element_type=F32)
        low = lax.dot_general(
            across[half:], weighted[half:], contract, preferred_element_type=F32
        )
        for k in range(slots):
            for l in range(k, slots):
                if k < slots // 2:
                    part = top[k * BLK : (k + 1) * BLK, l * BLK : (l + 1) * BLK]
                else:
                    i, j = k - slots // 2, l - slots // 2
                    part = low[i * BLK : (i + 1) * BLK, j * BLK : (j + 1) * BLK]
                total[homes[k], starts[l] - starts[k]] += part
        return carry

    lax.fori_loop(0, count, one, 0)


def batches(batch_blocks, weights, region, across, zeros):
    span = region.shape[3]
    near = pl.BlockSpec(memory_space=pltpu.VMEM)
    return pl.pallas_call(
        batch_kernel,
        name="batches",
        out_shape=(
            jax.ShapeDtypeStruct(weights.shape, F32),
            jax.ShapeDtypeStruct(zeros.shape, F32),
        ),
        in_specs=[pl.BlockSpec(memory_space=pltpu.SMEM)] + [near] * 4,
        out_specs=(near, near),
        input_output_aliases={4: 1},
        compiler_params=pltpu.CompilerParams(vmem_limit_bytes=12 * MIB),
    )(batch_blocks, across, weights, region.reshape(NZ * NX, NG, span, SLICE, BLK), zeros)


ORDER = (4, 3, -3, 2, -2, 1, -1, 0)
AHEAD = 3


def give_kernel(
    live_ref, lanes_ref, total_ref, out_ref,
    got, send, s4, s3r, s3l, s2r, s2l, s1r, s1l, i3r, i3l, i2r, i2l, i1r, i1l, i0r, i0l,
    plane_send, plane_recv, ring_send, ring_recv,
):
    y, c, z, x = place()
    me = slot_of(y, c, x)
    right, left = (y, c, (z + 1) % NZ, x), (y, c, (z + NZ - 1) % NZ, x)
    rows, span = out_ref.shape[:2]
    depth = rows * SLICE
    half = depth // 2
    greet(y, c, z, x)

    def hand(k):
        z_of = (z + ORDER[k] + NZ) % NZ
        for x2 in range(NX):
            for o in range(span):
                tile = total_ref[z_of * NX + x2, o].astype(BF16)
                send[k, x2, :, o] = tile.reshape(NG, SLICE, BLK)

        def one(i, carry):
            y2, c2, x2 = peer(i, y, c, x)
            remote(
                send.at[k, x2, y2 * NC + c2], got.at[k, me], plane_send.at[k],
                plane_recv.at[k], (y2, c2, z, x2),
            ).start()
            return carry

        lax.fori_loop(1, PLANE, one, 0)
        pltpu.make_async_copy(
            send.at[k, x, y * NC + c], got.at[k, me], plane_recv.at[k]
        ).start()

    lane = lax.broadcasted_iota(I32, lanes_ref.shape, 1) % SLICE
    first = lanes_ref[...]
    row_index = lax.broadcasted_iota(I32, (depth, PLANE * SLICE), 0)

    def partials(k):
        await_bytes(got.at[k], plane_recv.at[k])
        m = ((z + ORDER[k] + NZ) % NZ) * NX + x
        wanted = lax.shift_right_logical(first + ((m - first) & (NX * NZ - 1)), 5)
        key = (wanted * SLICE + lane)[0:1]
        chosen = jnp.where(row_index == key, 1.0, 0.0).astype(BF16)
        for o in range(span):
            block = got[k, :, o].reshape(PLANE * SLICE, BLK)
            yield o, jnp.dot(chosen, block, preferred_element_type=F32)

    def hop(n, src, dst, where):
        copy = remote(src, dst, ring_send.at[n], ring_recv.at[n], where)
        copy.start()
        return copy

    for k in range(AHEAD):
        hand(k)
    hops = []
    for o, part in partials(0):
        s4[o] = part.astype(BF16)
    hops.append(hop(0, s4.at[:, pl.ds(0, half)], i3r, right))
    hops.append(hop(1, s4.at[:, pl.ds(half, half)], i3l, left))
    chain = ((s3r, i3r, i2r), (s3l, i3l, i2l), (s2r, i2r, i1r), (s2l, i2l, i1l),
             (s1r, i1r, i0r), (s1l, i1l, i0l))
    for k, (mine, came, goes) in enumerate(chain, 1):
        if k + AHEAD - 1 < NZ:
            hand(k + AHEAD - 1)
        for o, part in partials(k):
            if o == 0:
                hops[k - 1].wait_recv()
            if k < 3:
                mine[o] = part.astype(BF16)
            if k == 1:
                mine[o, :half] = (part[:half] + came[o].astype(F32)).astype(BF16)
            elif k == 2:
                mine[o, half:] = (part[half:] + came[o].astype(F32)).astype(BF16)
            else:
                mine[o] = (part + came[o].astype(F32)).astype(BF16)
        hops.append(hop(k + 1, mine, goes, right if k % 2 else left))
    for o, part in partials(NZ - 1):
        if o == 0:
            hops[6].wait_recv()
            hops[7].wait_recv()
        total = part + i0r[o].astype(F32) + i0l[o].astype(F32)
        for t in range(rows):
            live = live_ref[t, o].astype(F32)
            out_ref[t, o] = (total[t * SLICE : (t + 1) * SLICE] * live).astype(BF16)
    for copy in hops:
        copy.wait_send()
    others = pl.ds(1, PLANE - 1)
    for k in range(NZ):
        await_bytes(got.at[k, others], plane_send.at[k])


def give(block_live, lanes, total):
    span, rows = total.shape[1], block_live.shape[0]
    sem = pltpu.SemaphoreType.DMA
    whole = pltpu.VMEM((span, rows * SLICE, BLK), BF16)
    part = pltpu.VMEM((span, rows * SLICE // 2, BLK), BF16)
    near = pl.BlockSpec(memory_space=pltpu.VMEM)
    return pl.pallas_call(
        give_kernel,
        name="give",
        out_shape=jax.ShapeDtypeStruct((rows, span, SLICE, BLK), BF16),
        in_specs=[pl.BlockSpec(memory_space=pltpu.SMEM), near, near],
        out_specs=near,
        scratch_shapes=[
            pltpu.VMEM((NZ, PLANE, span, SLICE, BLK), BF16),
            pltpu.VMEM((NZ, NX, NG, span, SLICE, BLK), BF16),
            *[whole] * 7,
            part, part, *[whole] * 6,
            sem((NZ,)), sem((NZ,)), sem((8,)), sem((8,)),
        ],
        compiler_params=pltpu.CompilerParams(
            collective_id=1, has_side_effects=True, vmem_limit_bytes=24 * MIB
        ),
    )(block_live, lanes, total)


def per_device(basis_values, weights, density, block_live, batch_blocks, live_functions):
    region, lanes, across, zeros = fetch(
        batch_blocks, block_live, live_functions, density, basis_values
    )
    site_density, total = batches(batch_blocks, weights, region, across, zeros)
    return site_density, give(block_live, lanes, total)


def solution(mesh):
    split = Mesh(mesh.devices.reshape(NY, NC, NZ, NX), AXES)
    placed = (
        P(AXES, None, None),
        P(AXES, None),
        P(MAT, None, None, None),
        P(MAT, None),
        P(AXES, None),
        P(AXES),
    )
    return jax.shard_map(
        per_device,
        mesh=split,
        in_specs=placed,
        out_specs=(P(AXES, None), P(MAT, None, GRP, None)),
        check_vma=False,
    )
```

```python
import jax
import jax.numpy as jnp
from jax import lax
from jax.experimental import pallas as pl
from jax.experimental.pallas import tpu as pltpu
from jax.sharding import Mesh
from jax.sharding import PartitionSpec as P

AXES = ("y", "c", "z", "x")
MAT = ("z", "x")
GRP = ("y", "c")
NX, NY, NZ, NC = 4, 4, 8, 2
NG = NY * NC
PLANE = NX * NG
BLK = 128
SLICE = BLK // NG
MESH = pl.DeviceIdType.MESH
MIB = 1 << 20
BF16, F32, I32 = jnp.bfloat16, jnp.float32, jnp.int32


def place():
    return tuple(lax.axis_index(a) for a in AXES)


def peer(i, y, c, x):
    return (y + (i // NX) % NY) % NY, (c + i // (NX * NY)) % NC, (x + i % NX) % NX


def slot_of(y, c, x):
    return x * NG + y * NC + c


def greet(y, c, z, x):
    barrier = pltpu.get_barrier_semaphore()

    def signal(i, carry):
        y2, c2, x2 = peer(i, y, c, x)
        pl.semaphore_signal(barrier, inc=1, device_id=(y2, c2, z, x2), device_id_type=MESH)
        return carry

    lax.fori_loop(1, PLANE, signal, 0)
    for step in (1, NZ - 1):
        pl.semaphore_signal(
            barrier, inc=1, device_id=(y, c, (z + step) % NZ, x), device_id_type=MESH
        )


def await_greetings():
    pl.semaphore_wait(pltpu.get_barrier_semaphore(), PLANE + 1)


def remote(src, dst, send_sem, recv_sem, where):
    return pltpu.make_async_remote_copy(
        src_ref=src,
        dst_ref=dst,
        send_sem=send_sem,
        recv_sem=recv_sem,
        device_id=where,
        device_id_type=MESH,
    )


def await_bytes(ref, sem):
    pltpu.make_async_copy(ref, ref, sem).wait()


def fetch_kernel(
    blocks_hbm, live_hbm, functions_hbm, density_ref, values_ref,
    region_ref, lanes_ref, across_ref, total_ref,
    own, r1, r2, r3, l1, l2, l3, far, send, first, firsts, row, firsts_s, blocks_ref, live_ref,
    functions_ref, raw,
    load_sem, first_send, first_recv, table_sem, small_sem, value_sem, ring_send, ring_recv,
    plane_send, plane_recv,
):
    y, c, z, x = place()
    g = y * NC + c
    me = slot_of(y, c, x)
    right, left = (y, c, (z + 1) % NZ, x), (y, c, (z + NZ - 1) % NZ, x)
    small = [
        pltpu.make_async_copy(blocks_hbm, blocks_ref, small_sem.at[0]),
        pltpu.make_async_copy(live_hbm, live_ref, small_sem.at[1]),
        pltpu.make_async_copy(functions_hbm, functions_ref, small_sem.at[2]),
    ]
    for copy in small:
        copy.start()
    load = pltpu.make_async_copy(density_ref.at[:, :, g], own, load_sem)
    load.start()
    greet(y, c, z, x)
    small[0].wait()
    first[...] = jnp.broadcast_to(jnp.min(blocks_ref[...], keepdims=True), first.shape)
    small[1].wait()
    small[2].wait()
    load.wait()
    rows, span = own.shape[:2]

    def mask(t, carry):
        for o in range(span):
            scale = live_ref[o, t].astype(F32) * (2.0 if o else 1.0)
            own[t, o] = own[t, o] * scale.astype(BF16)
        return carry

    lax.fori_loop(0, rows, mask, 0)
    await_greetings()

    def tell(i, carry):
        y2, c2, x2 = peer(i, y, c, x)
        remote(first, firsts.at[me], first_send, first_recv, (y2, c2, z, x2)).start()
        return carry

    lax.fori_loop(1, PLANE, tell, 0)
    pltpu.make_async_copy(first, firsts.at[me], first_recv).start()

    def hop(k, src, dst, where):
        copy = remote(src, dst, ring_send.at[k], ring_recv.at[k], where)
        copy.start()
        return copy

    half = rows // 2
    hop_r1 = hop(0, own, r1, right)
    hop_l1 = hop(1, own, l1, left)
    count = values_ref.shape[0]
    per = count // NZ

    def bring(b):
        slot = b % (2 * per)
        return pltpu.make_async_copy(values_ref.at[b], raw.at[slot], value_sem.at[slot])

    for b in range(per):
        bring(b).start()
    await_bytes(firsts, first_recv)
    lane = lax.broadcasted_iota(I32, (1, 128), 1)
    held = firsts[0]
    for d in range(1, PLANE):
        held = jnp.where(lane == d, firsts[d], held)
    row[...] = held
    table = pltpu.make_async_copy(row, firsts_s, table_sem)
    table.start()
    table.wait()

    def serve(k, source, z_of):
        m = z_of * NX + x

        def wanted(p):
            f = firsts_s[0, p]
            return lax.shift_right_logical(f + ((m - f) & (NX * NZ - 1)), 5)

        def one(i, carry):
            y2, c2, x2 = peer(i, y, c, x)
            send[k, i] = source[wanted(slot_of(y2, c2, x2))]
            remote(
                send.at[k, i], region_ref.at[z_of, x, g], plane_send.at[k], plane_recv.at[k],
                (y2, c2, z, x2),
            ).start()
            return carry

        lax.fori_loop(1, PLANE, one, 0)
        send[k, 0] = source[wanted(me)]
        pltpu.make_async_copy(send.at[k, 0], region_ref.at[z_of, x, g], plane_recv.at[k]).start()

    def prepare(k):
        for b in range(k * per, (k + 1) * per):
            if b + per < count:
                bring(b + per).start()
        for b in range(k * per, (k + 1) * per):
            bring(b).wait()
            across = raw[b % (2 * per)].T
            function_index = lax.broadcasted_iota(I32, across.shape, 0)
            across_ref[b] = jnp.where(
                function_index < functions_ref[b], across, jnp.zeros_like(across)
            )
        step = total_ref.shape[0] // NZ

        @pl.loop(k * step, (k + 1) * step)
        def _(m):
            total_ref[m] = jnp.zeros(total_ref.shape[1:], F32)

    serve(0, own, z)
    prepare(0)
    hop_r1.wait_recv()
    hop_r2 = hop(2, r1, r2, right)
    hop_l1.wait_recv()
    hop_l2 = hop(3, l1, l2, left)
    serve(1, r1, (z + NZ - 1) % NZ)
    serve(2, l1, (z + 1) % NZ)
    prepare(1)
    prepare(2)
    hop_r2.wait_recv()
    hop_r3 = hop(4, r2, r3, right)
    hop_l2.wait_recv()
    hop_l3 = hop(5, l2, l3, left)
    serve(3, r2, (z + NZ - 2) % NZ)
    serve(4, l2, (z + 2) % NZ)
    prepare(3)
    prepare(4)
    hop_r3.wait_recv()
    hop_rf = hop(6, r3.at[pl.ds(0, half)], far.at[pl.ds(0, half)], right)
    hop_l3.wait_recv()
    hop_lf = hop(7, l3.at[pl.ds(half, half)], far.at[pl.ds(half, half)], left)
    serve(5, r3, (z + NZ - 3) % NZ)
    serve(6, l3, (z + 3) % NZ)
    prepare(5)
    prepare(6)
    hop_rf.wait_recv()
    hop_lf.wait_recv()
    serve(7, far, (z + NZ // 2) % NZ)
    prepare(7)
    lane = lane // SLICE
    for chunk in range(PLANE * SLICE // 128):
        held = firsts[chunk * 8]
        for d in range(1, 8):
            held = jnp.where(lane == d, firsts[chunk * 8 + d], held)
        lanes_ref[:, chunk * 128 : (chunk + 1) * 128] = held
    for copy in (hop_r1, hop_l1, hop_r2, hop_l2, hop_r3, hop_l3, hop_rf, hop_lf):
        copy.wait_send()
    others = pl.ds(1, PLANE - 1)
    await_bytes(firsts.at[others], first_send)
    for k in range(NZ):
        await_bytes(send.at[k, others], plane_send.at[k])
    for k, off in enumerate((0, NZ - 1, 1, NZ - 2, 2, NZ - 3, 3, NZ // 2)):
        await_bytes(region_ref.at[(z + off) % NZ], plane_recv.at[k])


def fetch(batch_blocks, block_live, live_functions, density, basis_values):
    rows, span = density.shape[:2]
    count, points, width = basis_values.shape
    part = (rows, span, SLICE, BLK)
    sem = pltpu.SemaphoreType.DMA
    far_away = pl.BlockSpec(memory_space=pltpu.HBM)
    near = pl.BlockSpec(memory_space=pltpu.VMEM)
    return pl.pallas_call(
        fetch_kernel,
        name="fetch",
        out_shape=(
            jax.ShapeDtypeStruct((NZ, NX, NG, span, SLICE, BLK), BF16),
            jax.ShapeDtypeStruct((1, PLANE * SLICE), I32),
            jax.ShapeDtypeStruct((count, width, points), BF16),
            jax.ShapeDtypeStruct((NZ * NX, span, BLK, BLK), F32),
        ),
        in_specs=[far_away] * 5,
        out_specs=(near,) * 4,
        scratch_shapes=[
            *[pltpu.VMEM(part, BF16)] * 8,
            pltpu.VMEM((NZ, PLANE, span, SLICE, BLK), BF16),
            pltpu.VMEM((1, 128), I32),
            pltpu.VMEM((PLANE, 1, 128), I32),
            pltpu.VMEM((1, 128), I32),
            pltpu.SMEM((1, 128), I32),
            pltpu.VMEM(batch_blocks.shape, I32),
            pltpu.SMEM(block_live.shape, I32),
            pltpu.SMEM(live_functions.shape, I32),
            pltpu.VMEM((2 * count // NZ, points, width), BF16),
            sem, sem, sem, sem, sem((3,)), sem((2 * count // NZ,)), sem((8,)), sem((8,)),
            sem((NZ,)), sem((NZ,)),
        ],
        compiler_params=pltpu.CompilerParams(
            collective_id=0, has_side_effects=True, vmem_limit_bytes=16 * MIB
        ),
    )(
        *[
            pltpu.with_memory_space_constraint(a, pltpu.HBM)
            for a in (
                batch_blocks, block_live, live_functions,
                density.reshape(rows, span, NG, SLICE, BLK), basis_values,
            )
        ]
    )


def batch_kernel(blocks_ref, across_ref, weights_ref, region_ref, zeros_ref, site_ref, total):
    del zeros_ref
    slots, count = blocks_ref.shape
    half = slots * BLK // 2
    contract = (((1,), (1,)), ((), ()))

    def one(b):
        starts = [blocks_ref[k, b] for k in range(slots)]
        homes = [s & (NX * NZ - 1) for s in starts]
        across = across_ref[b]

        def tile(k, l):
            return region_ref[homes[k], :, starts[l] - starts[k]].reshape(BLK, BLK)

        wide = across.astype(F32)
        site = jnp.zeros((1, across.shape[1]), F32)
        for k in range(slots):
            tiles = jnp.concatenate([tile(k, l) for l in range(k, slots)], axis=1)
            product = jnp.dot(tiles, across[k * BLK :], preferred_element_type=F32)
            site += jnp.sum(product * wide[k * BLK : (k + 1) * BLK], axis=0, keepdims=True)
        site_ref[pl.ds(b, 1)] = site
        potential = weights_ref[pl.ds(b, 1)] * site / jnp.sqrt(1.0 + site * site)
        weighted = (potential * wide).astype(BF16)
        top = lax.dot_general(across[:half], weighted, contract, preferred_element_type=F32)
        low = lax.dot_general(
            across[half:], weighted[half:], contract, preferred_element_type=F32
        )
        return starts, homes, top, low

    def add(starts, homes, top, low):
        for k in range(slots):
            for l in range(k, slots):
                if k < slots // 2:
                    part = top[k * BLK : (k + 1) * BLK, l * BLK : (l + 1) * BLK]
                else:
                    i, j = k - slots // 2, l - slots // 2
                    part = low[i * BLK : (i + 1) * BLK, j * BLK : (j + 1) * BLK]
                total[homes[k], starts[l] - starts[k]] += part

    def some(i, carry):
        parts = [one(i * TOGETHER + j) for j in range(TOGETHER)]
        for part in parts:
            add(*part)
        return carry

    lax.fori_loop(0, count // TOGETHER, some, 0)


def batches(batch_blocks, weights, region, across, zeros):
    span = region.shape[3]
    near = pl.BlockSpec(memory_space=pltpu.VMEM)
    return pl.pallas_call(
        batch_kernel,
        name="batches",
        out_shape=(
            jax.ShapeDtypeStruct(weights.shape, F32),
            jax.ShapeDtypeStruct(zeros.shape, F32),
        ),
        in_specs=[pl.BlockSpec(memory_space=pltpu.SMEM)] + [near] * 4,
        out_specs=(near, near),
        input_output_aliases={4: 1},
        compiler_params=pltpu.CompilerParams(vmem_limit_bytes=12 * MIB),
    )(batch_blocks, across, weights, region.reshape(NZ * NX, NG, span, SLICE, BLK), zeros)


TOGETHER = 4
PIECES = (
    (4, 0, 5), (3, 0, 5), (-3, 0, 5), (2, 0, 5), (-2, 0, 5),
    (1, 0, 3), (-1, 0, 3), (1, 3, 5), (-1, 3, 5), (0, 0, 3), (0, 3, 5),
)
OFFS = (4, 3, -3, 2, -2, 1, -1, 0)
AHEAD = 3


def give_kernel(
    live_ref, lanes_ref, total_ref, out_ref,
    got, send, s4, s3r, s3l, s2r, s2l, s1r, s1l, i3r, i3l, i2r, i2l, i1r, i1l, i0r, i0l,
    plane_send, plane_recv, ring_send, ring_recv,
):
    y, c, z, x = place()
    me = slot_of(y, c, x)
    right, left = (y, c, (z + 1) % NZ, x), (y, c, (z + NZ - 1) % NZ, x)
    rows, span = out_ref.shape[:2]
    depth = rows * SLICE
    half = depth // 2
    greet(y, c, z, x)

    def pack(n):
        off, low, high = PIECES[n]
        z_of = (z + off + NZ) % NZ
        for x2 in range(NX):
            for o in range(low, high):
                tile = total_ref[z_of * NX + x2, o].astype(BF16)
                send[OFFS.index(off), x2, :, o] = tile.reshape(NG, SLICE, BLK)

    def hand(n):
        off, low, high = PIECES[n]
        k = OFFS.index(off)
        piece = pl.ds(low, high - low)

        def one(i, carry):
            y2, c2, x2 = peer(i, y, c, x)
            remote(
                send.at[k, x2, y2 * NC + c2, piece], got.at[k, me, piece], plane_send.at[n],
                plane_recv.at[n], (y2, c2, z, x2),
            ).start()
            return carry

        lax.fori_loop(1, PLANE, one, 0)
        pltpu.make_async_copy(
            send.at[k, x, y * NC + c, piece], got.at[k, me, piece], plane_recv.at[n]
        ).start()

    lane = lax.broadcasted_iota(I32, lanes_ref.shape, 1) % SLICE
    first = lanes_ref[...]
    row_index = lax.broadcasted_iota(I32, (depth, PLANE * SLICE), 0)

    def partials(n):
        off, low, high = PIECES[n]
        k = OFFS.index(off)
        await_bytes(got.at[k, :, pl.ds(low, high - low)], plane_recv.at[n])
        m = ((z + off + NZ) % NZ) * NX + x
        wanted = lax.shift_right_logical(first + ((m - first) & (NX * NZ - 1)), 5)
        key = wanted * SLICE + lane
        chosen = jnp.where(row_index == key, 1.0, 0.0).astype(BF16)
        for o in range(low, high):
            block = got[k, :, o].reshape(PLANE * SLICE, BLK)
            yield o, jnp.dot(chosen, block, preferred_element_type=F32)

    hops = {}
    waited = set()

    def hop(n, src, dst, where):
        place_of = len(hops)
        copy = remote(src, dst, ring_send.at[place_of], ring_recv.at[place_of], where)
        copy.start()
        hops[n] = copy

    pack(0)
    await_greetings()
    hand(0)
    for n in range(1, AHEAD):
        pack(n)
        hand(n)
    mine = {3: s3r, -3: s3l, 2: s2r, -2: s2l, 1: s1r, -1: s1l}
    came = {3: i3r, -3: i3l, 2: i2r, -2: i2l, 1: i1r, -1: i1l, 0: i0r}
    goes = {3: i2r, -3: i2l, 2: i1r, -2: i1l, 1: i0r, -1: i0l}
    for n, (off, low, high) in enumerate(PIECES):
        if n >= 1 and n + AHEAD - 1 < len(PIECES):
            pack(n + AHEAD - 1)
            hand(n + AHEAD - 1)
        piece = pl.ds(low, high - low)
        for o, part in partials(n):
            if off == 4:
                s4[o] = part.astype(BF16)
                continue
            if o == low:
                step = 1 if off > 0 else -1
                if off == 3 or off == -3:
                    hops[(4, step)].wait_recv()
                elif off:
                    for key in [q for q in hops if q[0] == off + step and q not in waited]:
                        hops[key].wait_recv()
                        waited.add(key)
                else:
                    for key in ((1, low), (-1, low)):
                        hops[key].wait_recv()
            if off == 3:
                mine[off][o, :half] = (part[:half] + came[off][o].astype(F32)).astype(BF16)
                mine[off][o, half:] = part[half:].astype(BF16)
            elif off == -3:
                mine[off][o, :half] = part[:half].astype(BF16)
                mine[off][o, half:] = (part[half:] + came[off][o].astype(F32)).astype(BF16)
            elif off:
                mine[off][o] = (part + came[off][o].astype(F32)).astype(BF16)
            else:
                total = part + i0r[o].astype(F32) + i0l[o].astype(F32)
                for t in range(rows):
                    live = live_ref[o, t].astype(F32)
                    out_ref[t, o] = (total[t * SLICE : (t + 1) * SLICE] * live).astype(BF16)
        if off == 4:
            hop((4, 1), s4.at[:, pl.ds(0, half)], i3r, right)
            hop((4, -1), s4.at[:, pl.ds(half, half)], i3l, left)
        elif off:
            hop((off, low), mine[off].at[piece], goes[off].at[piece], right if off > 0 else left)
    for copy in hops.values():
        copy.wait_send()
    others = pl.ds(1, PLANE - 1)
    for n, (off, low, high) in enumerate(PIECES):
        await_bytes(got.at[OFFS.index(off), others, pl.ds(low, high - low)], plane_send.at[n])


def give(block_live, lanes, total):
    span, rows = total.shape[1], block_live.shape[1]
    sem = pltpu.SemaphoreType.DMA
    whole = pltpu.VMEM((span, rows * SLICE, BLK), BF16)
    part = pltpu.VMEM((span, rows * SLICE // 2, BLK), BF16)
    near = pl.BlockSpec(memory_space=pltpu.VMEM)
    return pl.pallas_call(
        give_kernel,
        name="give",
        out_shape=jax.ShapeDtypeStruct((rows, span, SLICE, BLK), BF16),
        in_specs=[pl.BlockSpec(memory_space=pltpu.SMEM), near, near],
        out_specs=near,
        scratch_shapes=[
            pltpu.VMEM((NZ, PLANE, span, SLICE, BLK), BF16),
            pltpu.VMEM((NZ, NX, NG, span, SLICE, BLK), BF16),
            *[whole] * 7,
            part, part, *[whole] * 6,
            sem((len(PIECES),)), sem((len(PIECES),)), sem((10,)), sem((10,)),
        ],
        compiler_params=pltpu.CompilerParams(
            collective_id=1, has_side_effects=True, vmem_limit_bytes=24 * MIB
        ),
    )(block_live, lanes, total)


def per_device(basis_values, weights, density, block_live, batch_blocks, live_functions):
    batch_blocks, block_live = batch_blocks.T, block_live.T
    region, lanes, across, zeros = fetch(
        batch_blocks, block_live, live_functions, density, basis_values
    )
    site_density, total = batches(batch_blocks, weights, region, across, zeros)
    return site_density, give(block_live, lanes, total)


def solution(mesh):
    split = Mesh(mesh.devices.reshape(NY, NC, NZ, NX), AXES)
    placed = (
        P(AXES, None, None),
        P(AXES, None),
        P(MAT, None, None, None),
        P(MAT, None),
        P(AXES, None),
        P(AXES),
    )
    return jax.shard_map(
        per_device,
        mesh=split,
        in_specs=placed,
        out_specs=(P(AXES, None), P(MAT, None, GRP, None)),
        check_vma=False,
    )
```

```python
import jax
import jax.numpy as jnp
from jax import lax
from jax.experimental import pallas as pl
from jax.experimental.pallas import tpu as pltpu
from jax.sharding import Mesh
from jax.sharding import PartitionSpec as P

AXES = ("y", "c", "z", "x")
MAT = ("z", "x")
GRP = ("y", "c")
NX, NY, NZ, NC = 4, 4, 8, 2
NG = NY * NC
PLANE = NX * NG
BLK = 128
SLICE = BLK // NG
MESH = pl.DeviceIdType.MESH
MIB = 1 << 20
BF16, F32, I32 = jnp.bfloat16, jnp.float32, jnp.int32


def place():
    return tuple(lax.axis_index(a) for a in AXES)


def peer(i, y, c, x):
    row = lax.div(i, NX)
    return (
        lax.rem(y + lax.rem(row, NY), NY),
        lax.rem(c + lax.div(row, NY), NC),
        lax.rem(x + lax.rem(i, NX), NX),
    )


def slot_of(y, c, x):
    return x * NG + y * NC + c


def greet(y, c, z, x):
    barrier = pltpu.get_barrier_semaphore()

    def signal(i, carry):
        y2, c2, x2 = peer(i, y, c, x)
        pl.semaphore_signal(barrier, inc=1, device_id=(y2, c2, z, x2), device_id_type=MESH)
        return carry

    lax.fori_loop(1, PLANE, signal, 0, unroll=True)
    for step in (1, NZ - 1):
        pl.semaphore_signal(
            barrier, inc=1, device_id=(y, c, (z + step) % NZ, x), device_id_type=MESH
        )


def await_greetings():
    pl.semaphore_wait(pltpu.get_barrier_semaphore(), PLANE + 1)


def remote(src, dst, send_sem, recv_sem, where):
    return pltpu.make_async_remote_copy(
        src_ref=src,
        dst_ref=dst,
        send_sem=send_sem,
        recv_sem=recv_sem,
        device_id=where,
        device_id_type=MESH,
    )


def await_bytes(ref, sem):
    pltpu.make_async_copy(ref, ref, sem).wait()


def fetch_kernel(
    blocks_hbm, live_hbm, functions_hbm, density_ref, values_ref,
    region_ref, lanes_ref, across_ref, total_ref,
    own, r1, r2, r3, l1, l2, l3, far, send, first, firsts, row, firsts_s, blocks_ref, live_ref,
    functions_ref, raw,
    load_sem, first_send, first_recv, table_sem, small_sem, value_sem, ring_send, ring_recv,
    plane_send, plane_recv,
):
    y, c, z, x = place()
    g = y * NC + c
    me = slot_of(y, c, x)
    right, left = (y, c, (z + 1) % NZ, x), (y, c, (z + NZ - 1) % NZ, x)
    small = [
        pltpu.make_async_copy(blocks_hbm, blocks_ref, small_sem.at[0]),
        pltpu.make_async_copy(live_hbm, live_ref, small_sem.at[1]),
        pltpu.make_async_copy(functions_hbm, functions_ref, small_sem.at[2]),
    ]
    for copy in small:
        copy.start()
    load = pltpu.make_async_copy(density_ref.at[:, :, g], own, load_sem)
    load.start()
    greet(y, c, z, x)
    small[0].wait()
    first[...] = jnp.broadcast_to(jnp.min(blocks_ref[...], keepdims=True), first.shape)
    small[1].wait()
    small[2].wait()
    load.wait()
    rows, span = own.shape[:2]

    def mask(t, carry):
        for o in range(span):
            scale = live_ref[o, t].astype(F32) * (2.0 if o else 1.0)
            own[t, o] = own[t, o] * scale.astype(BF16)
        return carry

    lax.fori_loop(0, rows, mask, 0)
    await_greetings()

    def tell(i, carry):
        y2, c2, x2 = peer(i, y, c, x)
        remote(first, firsts.at[me], first_send, first_recv, (y2, c2, z, x2)).start()
        return carry

    lax.fori_loop(1, PLANE, tell, 0, unroll=True)
    pltpu.make_async_copy(first, firsts.at[me], first_recv).start()

    def hop(k, src, dst, where):
        copy = remote(src, dst, ring_send.at[k], ring_recv.at[k], where)
        copy.start()
        return copy

    half = rows // 2
    hop_r1 = hop(0, own, r1, right)
    hop_l1 = hop(1, own, l1, left)
    count = values_ref.shape[0]
    per = count // NZ

    def bring(b):
        slot = b % (2 * per)
        return pltpu.make_async_copy(values_ref.at[b], raw.at[slot], value_sem.at[slot])

    for b in range(per):
        bring(b).start()
    await_bytes(firsts, first_recv)
    lane = lax.broadcasted_iota(I32, (1, 128), 1)
    held = firsts[0]
    for d in range(1, PLANE):
        held = jnp.where(lane == d, firsts[d], held)
    row[...] = held
    table = pltpu.make_async_copy(row, firsts_s, table_sem)
    table.start()
    table.wait()

    def serve(k, source, z_of):
        m = z_of * NX + x

        def wanted(p):
            f = firsts_s[0, p]
            return lax.shift_right_logical(f + ((m - f) & (NX * NZ - 1)), 5)

        def one(i, carry):
            y2, c2, x2 = peer(i, y, c, x)
            send[k, i] = source[wanted(slot_of(y2, c2, x2))]
            remote(
                send.at[k, i], region_ref.at[z_of, x, g], plane_send.at[k], plane_recv.at[k],
                (y2, c2, z, x2),
            ).start()
            return carry

        lax.fori_loop(1, PLANE, one, 0)
        send[k, 0] = source[wanted(me)]
        pltpu.make_async_copy(send.at[k, 0], region_ref.at[z_of, x, g], plane_recv.at[k]).start()

    def prepare(k):
        for b in range(k * per, (k + 1) * per):
            if b + per < count:
                bring(b + per).start()
        for b in range(k * per, (k + 1) * per):
            bring(b).wait()
            across = raw[b % (2 * per)].T
            function_index = lax.broadcasted_iota(I32, across.shape, 0)
            across_ref[b] = jnp.where(
                function_index < functions_ref[b], across, jnp.zeros_like(across)
            )
        step = total_ref.shape[0] // NZ

        @pl.loop(k * step, (k + 1) * step)
        def _(m):
            total_ref[m] = jnp.zeros(total_ref.shape[1:], F32)

    serve(0, own, z)
    prepare(0)
    hop_r1.wait_recv()
    hop_r2 = hop(2, r1, r2, right)
    hop_l1.wait_recv()
    hop_l2 = hop(3, l1, l2, left)
    serve(1, r1, (z + NZ - 1) % NZ)
    serve(2, l1, (z + 1) % NZ)
    prepare(1)
    prepare(2)
    hop_r2.wait_recv()
    hop_r3 = hop(4, r2, r3, right)
    hop_l2.wait_recv()
    hop_l3 = hop(5, l2, l3, left)
    serve(3, r2, (z + NZ - 2) % NZ)
    serve(4, l2, (z + 2) % NZ)
    prepare(3)
    prepare(4)
    hop_r3.wait_recv()
    hop_rf = hop(6, r3.at[pl.ds(0, half)], far.at[pl.ds(0, half)], right)
    hop_l3.wait_recv()
    hop_lf = hop(7, l3.at[pl.ds(half, half)], far.at[pl.ds(half, half)], left)
    serve(5, r3, (z + NZ - 3) % NZ)
    serve(6, l3, (z + 3) % NZ)
    prepare(5)
    prepare(6)
    hop_rf.wait_recv()
    hop_lf.wait_recv()
    serve(7, far, (z + NZ // 2) % NZ)
    prepare(7)
    lane = lane // SLICE
    for chunk in range(PLANE * SLICE // 128):
        held = firsts[chunk * 8]
        for d in range(1, 8):
            held = jnp.where(lane == d, firsts[chunk * 8 + d], held)
        lanes_ref[:, chunk * 128 : (chunk + 1) * 128] = held
    for copy in (hop_r1, hop_l1, hop_r2, hop_l2, hop_r3, hop_l3, hop_rf, hop_lf):
        copy.wait_send()
    others = pl.ds(1, PLANE - 1)
    await_bytes(firsts.at[others], first_send)
    for k in range(NZ):
        await_bytes(send.at[k, others], plane_send.at[k])
    for k, off in enumerate((0, NZ - 1, 1, NZ - 2, 2, NZ - 3, 3, NZ // 2)):
        await_bytes(region_ref.at[(z + off) % NZ], plane_recv.at[k])


def fetch(batch_blocks, block_live, live_functions, density, basis_values):
    rows, span = density.shape[:2]
    count, points, width = basis_values.shape
    part = (rows, span, SLICE, BLK)
    sem = pltpu.SemaphoreType.DMA
    far_away = pl.BlockSpec(memory_space=pltpu.HBM)
    near = pl.BlockSpec(memory_space=pltpu.VMEM)
    return pl.pallas_call(
        fetch_kernel,
        name="fetch",
        out_shape=(
            jax.ShapeDtypeStruct((NZ, NX, NG, span, SLICE, BLK), BF16),
            jax.ShapeDtypeStruct((1, PLANE * SLICE), I32),
            jax.ShapeDtypeStruct((count, width, points), BF16),
            jax.ShapeDtypeStruct((NZ * NX, span, BLK, BLK), F32),
        ),
        in_specs=[far_away] * 5,
        out_specs=(near,) * 4,
        scratch_shapes=[
            *[pltpu.VMEM(part, BF16)] * 8,
            pltpu.VMEM((NZ, PLANE, span, SLICE, BLK), BF16),
            pltpu.VMEM((1, 128), I32),
            pltpu.VMEM((PLANE, 1, 128), I32),
            pltpu.VMEM((1, 128), I32),
            pltpu.SMEM((1, 128), I32),
            pltpu.VMEM(batch_blocks.shape, I32),
            pltpu.SMEM(block_live.shape, I32),
            pltpu.SMEM(live_functions.shape, I32),
            pltpu.VMEM((2 * count // NZ, points, width), BF16),
            sem, sem, sem, sem, sem((3,)), sem((2 * count // NZ,)), sem((8,)), sem((8,)),
            sem((NZ,)), sem((NZ,)),
        ],
        compiler_params=pltpu.CompilerParams(
            collective_id=0, has_side_effects=True, vmem_limit_bytes=16 * MIB
        ),
    )(
        *[
            pltpu.with_memory_space_constraint(a, pltpu.HBM)
            for a in (
                batch_blocks, block_live, live_functions,
                density.reshape(rows, span, NG, SLICE, BLK), basis_values,
            )
        ]
    )


def batch_kernel(blocks_ref, across_ref, weights_ref, region_ref, zeros_ref, site_ref, total):
    del zeros_ref
    slots, count = blocks_ref.shape
    half = slots * BLK // 2
    contract = (((1,), (1,)), ((), ()))

    def one(b):
        starts = [blocks_ref[k, b] for k in range(slots)]
        homes = [s & (NX * NZ - 1) for s in starts]
        across = across_ref[b]

        def tile(k, l):
            return region_ref[homes[k], :, starts[l] - starts[k]].reshape(BLK, BLK)

        wide = across.astype(F32)
        site = jnp.zeros((1, across.shape[1]), F32)
        for k in range(slots):
            tiles = jnp.concatenate([tile(k, l) for l in range(k, slots)], axis=1)
            product = jnp.dot(tiles, across[k * BLK :], preferred_element_type=F32)
            site += jnp.sum(product * wide[k * BLK : (k + 1) * BLK], axis=0, keepdims=True)
        site_ref[pl.ds(b, 1)] = site
        potential = weights_ref[pl.ds(b, 1)] * site / jnp.sqrt(1.0 + site * site)
        weighted = (potential * wide).astype(BF16)
        top = lax.dot_general(across[:half], weighted, contract, preferred_element_type=F32)
        low = lax.dot_general(
            across[half:], weighted[half:], contract, preferred_element_type=F32
        )
        return starts, homes, top, low

    def add(starts, homes, top, low):
        for k in range(slots):
            for l in range(k, slots):
                if k < slots // 2:
                    part = top[k * BLK : (k + 1) * BLK, l * BLK : (l + 1) * BLK]
                else:
                    i, j = k - slots // 2, l - slots // 2
                    part = low[i * BLK : (i + 1) * BLK, j * BLK : (j + 1) * BLK]
                total[homes[k], starts[l] - starts[k]] += part

    def some(i, carry):
        parts = [one(i * TOGETHER + j) for j in range(TOGETHER)]
        for part in parts:
            add(*part)
        return carry

    lax.fori_loop(0, count // TOGETHER, some, 0)


def batches(batch_blocks, weights, region, across, zeros):
    span = region.shape[3]
    near = pl.BlockSpec(memory_space=pltpu.VMEM)
    return pl.pallas_call(
        batch_kernel,
        name="batches",
        out_shape=(
            jax.ShapeDtypeStruct(weights.shape, F32),
            jax.ShapeDtypeStruct(zeros.shape, F32),
        ),
        in_specs=[pl.BlockSpec(memory_space=pltpu.SMEM)] + [near] * 4,
        out_specs=(near, near),
        input_output_aliases={4: 1},
        compiler_params=pltpu.CompilerParams(vmem_limit_bytes=12 * MIB),
    )(batch_blocks, across, weights, region.reshape(NZ * NX, NG, span, SLICE, BLK), zeros)


TOGETHER = 8
PIECES = (
    (4, 0, 3), (4, 3, 5), (3, 0, 3), (-3, 0, 3), (3, 3, 5), (-3, 3, 5), (2, 0, 3), (-2, 0, 3), (2, 3, 5), (-2, 3, 5), (1, 0, 3), (-1, 0, 3), (1, 3, 5), (-1, 3, 5), (0, 0, 3), (0, 3, 5),
)
HOPS = sum(1 if 0 < abs(off) < 4 else off // 2 for off, _, _ in PIECES)
OFFS = (4, 3, -3, 2, -2, 1, -1, 0)
AHEAD = 4


def give_kernel(
    live_ref, lanes_ref, total_ref, out_ref,
    got, send, s4, s3r, s3l, s2r, s2l, s1r, s1l, i3r, i3l, i2r, i2l, i1r, i1l, i0r, i0l,
    plane_send, plane_recv, ring_send, ring_recv,
):
    y, c, z, x = place()
    me = slot_of(y, c, x)
    right, left = (y, c, (z + 1) % NZ, x), (y, c, (z + NZ - 1) % NZ, x)
    rows, span = out_ref.shape[:2]
    depth = rows * SLICE
    half = depth // 2
    greet(y, c, z, x)

    def pack(n):
        off, low, high = PIECES[n]
        z_of = (z + off + NZ) % NZ
        for x2 in range(NX):
            for o in range(low, high):
                tile = total_ref[z_of * NX + x2, o].astype(BF16)
                send[OFFS.index(off), x2, :, o] = tile.reshape(NG, SLICE, BLK)

    def hand(n):
        off, low, high = PIECES[n]
        k = OFFS.index(off)
        piece = pl.ds(low, high - low)

        def one(i, carry):
            y2, c2, x2 = peer(i, y, c, x)
            remote(
                send.at[k, x2, y2 * NC + c2, piece], got.at[k, me, piece], plane_send.at[n],
                plane_recv.at[n], (y2, c2, z, x2),
            ).start()
            return carry

        lax.fori_loop(1, PLANE, one, 0)
        pltpu.make_async_copy(
            send.at[k, x, y * NC + c, piece], got.at[k, me, piece], plane_recv.at[n]
        ).start()

    lane = lax.broadcasted_iota(I32, lanes_ref.shape, 1) % SLICE
    first = lanes_ref[...]
    row_index = lax.broadcasted_iota(I32, (depth, PLANE * SLICE), 0)

    def partials(n):
        off, low, high = PIECES[n]
        k = OFFS.index(off)
        await_bytes(got.at[k, :, pl.ds(low, high - low)], plane_recv.at[n])
        m = ((z + off + NZ) % NZ) * NX + x
        wanted = lax.shift_right_logical(first + ((m - first) & (NX * NZ - 1)), 5)
        key = wanted * SLICE + lane
        chosen = jnp.where(row_index == key, 1.0, 0.0).astype(BF16)
        for o in range(low, high):
            block = got[k, :, o].reshape(PLANE * SLICE, BLK)
            yield o, jnp.dot(chosen, block, preferred_element_type=F32)

    hops = {}
    waited = set()

    def hop(n, src, dst, where):
        place_of = len(hops)
        copy = remote(src, dst, ring_send.at[place_of], ring_recv.at[place_of], where)
        copy.start()
        hops[n] = copy

    pack(0)
    await_greetings()
    hand(0)
    for n in range(1, AHEAD):
        pack(n)
        hand(n)
    mine = {3: s3r, -3: s3l, 2: s2r, -2: s2l, 1: s1r, -1: s1l}
    came = {3: i3r, -3: i3l, 2: i2r, -2: i2l, 1: i1r, -1: i1l, 0: i0r}
    goes = {3: i2r, -3: i2l, 2: i1r, -2: i1l, 1: i0r, -1: i0l}
    for n, (off, low, high) in enumerate(PIECES):
        if n >= 1 and n + AHEAD - 1 < len(PIECES):
            pack(n + AHEAD - 1)
            hand(n + AHEAD - 1)
        piece = pl.ds(low, high - low)
        for o, part in partials(n):
            if off == 4:
                s4[o] = part.astype(BF16)
                continue
            if o == low:
                sources = [(4 if off == -3 else off + step, step) for step in (1, -1) if off * step >= 0]
                for key in list(hops):
                    near = key[:2] in sources and key[2] < high and key[3] > low
                    if near and key not in waited:
                        hops[key].wait_recv()
                        waited.add(key)
            if off == 3:
                mine[off][o, :half] = (part[:half] + came[off][o].astype(F32)).astype(BF16)
                mine[off][o, half:] = part[half:].astype(BF16)
            elif off == -3:
                mine[off][o, :half] = part[:half].astype(BF16)
                mine[off][o, half:] = (part[half:] + came[off][o].astype(F32)).astype(BF16)
            elif off:
                mine[off][o] = (part + came[off][o].astype(F32)).astype(BF16)
            else:
                total = part + i0r[o].astype(F32) + i0l[o].astype(F32)
                for t in range(rows):
                    live = live_ref[o, t].astype(F32)
                    out_ref[t, o] = (total[t * SLICE : (t + 1) * SLICE] * live).astype(BF16)
        if off == 4:
            top, low_half = pl.ds(0, half), pl.ds(half, half)
            hop((4, 1, low, high), s4.at[piece, top], i3r.at[piece], right)
            hop((4, -1, low, high), s4.at[piece, low_half], i3l.at[piece], left)
        elif off:
            step = 1 if off > 0 else -1
            where = right if off > 0 else left
            hop((off, step, low, high), mine[off].at[piece], goes[off].at[piece], where)
    for copy in hops.values():
        copy.wait_send()
    others = pl.ds(1, PLANE - 1)
    for n, (off, low, high) in enumerate(PIECES):
        await_bytes(got.at[OFFS.index(off), others, pl.ds(low, high - low)], plane_send.at[n])


def give(block_live, lanes, total):
    span, rows = total.shape[1], block_live.shape[1]
    sem = pltpu.SemaphoreType.DMA
    whole = pltpu.VMEM((span, rows * SLICE, BLK), BF16)
    part = pltpu.VMEM((span, rows * SLICE // 2, BLK), BF16)
    near = pl.BlockSpec(memory_space=pltpu.VMEM)
    return pl.pallas_call(
        give_kernel,
        name="give",
        out_shape=jax.ShapeDtypeStruct((rows, span, SLICE, BLK), BF16),
        in_specs=[pl.BlockSpec(memory_space=pltpu.SMEM), near, near],
        out_specs=near,
        scratch_shapes=[
            pltpu.VMEM((NZ, PLANE, span, SLICE, BLK), BF16),
            pltpu.VMEM((NZ, NX, NG, span, SLICE, BLK), BF16),
            *[whole] * 7,
            part, part, *[whole] * 6,
            sem((len(PIECES),)), sem((len(PIECES),)), sem((HOPS,)), sem((HOPS,)),
        ],
        compiler_params=pltpu.CompilerParams(
            collective_id=1, has_side_effects=True, vmem_limit_bytes=24 * MIB
        ),
    )(block_live, lanes, total)


def per_device(basis_values, weights, density, block_live, batch_blocks, live_functions):
    batch_blocks, block_live = batch_blocks.T, block_live.T
    region, lanes, across, zeros = fetch(
        batch_blocks, block_live, live_functions, density, basis_values
    )
    site_density, total = batches(batch_blocks, weights, region, across, zeros)
    return site_density, give(block_live, lanes, total)


def solution(mesh):
    split = Mesh(mesh.devices.reshape(NY, NC, NZ, NX), AXES)
    placed = (
        P(AXES, None, None),
        P(AXES, None),
        P(MAT, None, None, None),
        P(MAT, None),
        P(AXES, None),
        P(AXES),
    )
    return jax.shard_map(
        per_device,
        mesh=split,
        in_specs=placed,
        out_specs=(P(AXES, None), P(MAT, None, GRP, None)),
        check_vma=False,
    )
```

```python
import jax
import jax.numpy as jnp
from jax import lax
from jax.experimental import pallas as pl
from jax.experimental.pallas import tpu as pltpu
from jax.sharding import Mesh
from jax.sharding import PartitionSpec as P

AXES = ("y", "c", "z", "x")
MAT = ("z", "x")
GRP = ("y", "c")
NX, NY, NZ, NC = 4, 4, 8, 2
NG = NY * NC
PLANE = NX * NG
BLK = 128
SLICE = BLK // NG
MESH = pl.DeviceIdType.MESH
MIB = 1 << 20
BF16, F32, I32 = jnp.bfloat16, jnp.float32, jnp.int32


def place():
    return tuple(lax.axis_index(a) for a in AXES)


def peer(i, y, c, x):
    row = lax.div(i, NX)
    return (
        lax.rem(y + lax.rem(row, NY), NY),
        lax.rem(c + lax.div(row, NY), NC),
        lax.rem(x + lax.rem(i, NX), NX),
    )


def slot_of(y, c, x):
    return x * NG + y * NC + c


def greet(y, c, z, x):
    barrier = pltpu.get_barrier_semaphore()

    def signal(i, carry):
        y2, c2, x2 = peer(i, y, c, x)
        pl.semaphore_signal(barrier, inc=1, device_id=(y2, c2, z, x2), device_id_type=MESH)
        return carry

    lax.fori_loop(1, PLANE, signal, 0, unroll=True)
    for step in (1, NZ - 1):
        pl.semaphore_signal(
            barrier, inc=1, device_id=(y, c, (z + step) % NZ, x), device_id_type=MESH
        )


def await_greetings():
    pl.semaphore_wait(pltpu.get_barrier_semaphore(), PLANE + 1)


def remote(src, dst, send_sem, recv_sem, where):
    return pltpu.make_async_remote_copy(
        src_ref=src,
        dst_ref=dst,
        send_sem=send_sem,
        recv_sem=recv_sem,
        device_id=where,
        device_id_type=MESH,
    )


def await_bytes(ref, sem):
    pltpu.make_async_copy(ref, ref, sem).wait()


PARTS = ((0, 3), (3, 5))


def fetch_kernel(
    blocks_hbm, live_hbm, functions_hbm, density_ref, values_ref,
    region_ref, lanes_ref, across_ref, total_ref,
    own_a, own_b, r1_a, r1_b, r2_a, r2_b, r3_a, r3_b, l1_a, l1_b, l2_a, l2_b, l3_a, l3_b,
    far_a, far_b, send, first, firsts, row, firsts_s, blocks_ref, live_ref,
    functions_ref, raw,
    load_sem, first_send, first_recv, table_sem, small_sem, value_sem, ring_send, ring_recv,
    plane_send, plane_recv,
):
    y, c, z, x = place()
    g = y * NC + c
    me = slot_of(y, c, x)
    right, left = (y, c, (z + 1) % NZ, x), (y, c, (z + NZ - 1) % NZ, x)
    small = [
        pltpu.make_async_copy(blocks_hbm, blocks_ref, small_sem.at[0]),
        pltpu.make_async_copy(live_hbm, live_ref, small_sem.at[1]),
        pltpu.make_async_copy(functions_hbm, functions_ref, small_sem.at[2]),
    ]
    for copy in small:
        copy.start()
    own, far = (own_a, own_b), (far_a, far_b)
    r1, r2, r3 = (r1_a, r1_b), (r2_a, r2_b), (r3_a, r3_b)
    l1, l2, l3 = (l1_a, l1_b), (l2_a, l2_b), (l3_a, l3_b)
    loads = [
        pltpu.make_async_copy(density_ref.at[:, pl.ds(low, high - low), g], part, load_sem.at[p])
        for p, ((low, high), part) in enumerate(zip(PARTS, own))
    ]
    for load in loads:
        load.start()
    greet(y, c, z, x)
    small[0].wait()
    first[...] = jnp.broadcast_to(jnp.min(blocks_ref[...], keepdims=True), first.shape)
    small[1].wait()
    small[2].wait()
    for load in loads:
        load.wait()
    rows = own_a.shape[0]

    def mask(t, carry):
        for (low, high), part in zip(PARTS, own):
            for o in range(low, high):
                scale = live_ref[o, t].astype(F32) * (2.0 if o else 1.0)
                part[t, o - low] = part[t, o - low] * scale.astype(BF16)
        return carry

    lax.fori_loop(0, rows, mask, 0)
    await_greetings()

    def tell(i, carry):
        y2, c2, x2 = peer(i, y, c, x)
        remote(first, firsts.at[me], first_send, first_recv, (y2, c2, z, x2)).start()
        return carry

    lax.fori_loop(1, PLANE, tell, 0, unroll=True)
    pltpu.make_async_copy(first, firsts.at[me], first_recv).start()

    hops = []

    def hop(src, dst, where):
        k = len(hops)
        copy = remote(src, dst, ring_send.at[k], ring_recv.at[k], where)
        copy.start()
        hops.append(copy)
        return copy

    half = rows // 2
    first_hops = [(hop(own[p], r1[p], right), hop(own[p], l1[p], left)) for p in range(2)]
    count = values_ref.shape[0]
    per = count // NZ

    def bring(b):
        slot = b % (2 * per)
        return pltpu.make_async_copy(values_ref.at[b], raw.at[slot], value_sem.at[slot])

    for b in range(per):
        bring(b).start()
    await_bytes(firsts, first_recv)
    lane = lax.broadcasted_iota(I32, (1, 128), 1)
    held = firsts[0]
    for d in range(1, PLANE):
        held = jnp.where(lane == d, firsts[d], held)
    row[...] = held
    table = pltpu.make_async_copy(row, firsts_s, table_sem)
    table.start()
    table.wait()

    def serve(k, p, source, z_of):
        m = z_of * NX + x
        low, high = PARTS[p]
        piece = pl.ds(low, high - low)

        def wanted(d):
            f = firsts_s[0, d]
            return lax.shift_right_logical(f + ((m - f) & (NX * NZ - 1)), 5)

        def one(i, carry):
            y2, c2, x2 = peer(i, y, c, x)
            send[k, i, low:high] = source[p][wanted(slot_of(y2, c2, x2))]
            remote(
                send.at[k, i, piece], region_ref.at[z_of, x, g, piece], plane_send.at[2 * k + p],
                plane_recv.at[2 * k + p], (y2, c2, z, x2),
            ).start()
            return carry

        lax.fori_loop(1, PLANE, one, 0)
        send[k, 0, low:high] = source[p][wanted(me)]
        pltpu.make_async_copy(
            send.at[k, 0, piece], region_ref.at[z_of, x, g, piece], plane_recv.at[2 * k + p]
        ).start()

    def prepare(k):
        for b in range(k * per, (k + 1) * per):
            if b + per < count:
                bring(b + per).start()
        for b in range(k * per, (k + 1) * per):
            bring(b).wait()
            across = raw[b % (2 * per)].T
            function_index = lax.broadcasted_iota(I32, across.shape, 0)
            across_ref[b] = jnp.where(
                function_index < functions_ref[b], across, jnp.zeros_like(across)
            )
        step = total_ref.shape[0] // NZ

        @pl.loop(k * step, (k + 1) * step)
        def _(m):
            total_ref[m] = jnp.zeros(total_ref.shape[1:], F32)

    serve(0, 0, own, z)
    serve(0, 1, own, z)
    prepare(0)
    came = first_hops
    for step, (rs, ls, rd, ld) in enumerate(((r1, l1, r2, l2), (r2, l2, r3, l3), (r3, l3, far, far)), 1):
        goes = []
        for p in range(2):
            for side in range(2):
                came[p][side].wait_recv()
                source, target, where = ((rs, rd, right), (ls, ld, left))[side]
                source, target = source[p], target[p]
                if step == 3:
                    rows_of = pl.ds(side * half, half)
                    source, target = source.at[rows_of], target.at[rows_of]
                goes.append(hop(source, target, where))
            serve(2 * step - 1, p, rs, (z + NZ - step) % NZ)
            serve(2 * step, p, ls, (z + step) % NZ)
        came = [goes[:2], goes[2:]]
        prepare(2 * step - 1)
        prepare(2 * step)
    for p in range(2):
        came[p][0].wait_recv()
        came[p][1].wait_recv()
        serve(7, p, far, (z + NZ // 2) % NZ)
    prepare(7)
    lane = lane // SLICE
    for chunk in range(PLANE * SLICE // 128):
        held = firsts[chunk * 8]
        for d in range(1, 8):
            held = jnp.where(lane == d, firsts[chunk * 8 + d], held)
        lanes_ref[:, chunk * 128 : (chunk + 1) * 128] = held
    for copy in hops:
        copy.wait_send()
    others = pl.ds(1, PLANE - 1)
    await_bytes(firsts.at[others], first_send)
    for k, off in enumerate((0, NZ - 1, 1, NZ - 2, 2, NZ - 3, 3, NZ // 2)):
        for p, (low, high) in enumerate(PARTS):
            piece = pl.ds(low, high - low)
            await_bytes(send.at[k, others, piece], plane_send.at[2 * k + p])
            arrived = region_ref.at[(z + off) % NZ, :, :, piece]
            await_bytes(arrived, plane_recv.at[2 * k + p])


def fetch(batch_blocks, block_live, live_functions, density, basis_values):
    rows, span = density.shape[:2]
    count, points, width = basis_values.shape
    part = [pltpu.VMEM((rows, high - low, SLICE, BLK), BF16) for low, high in PARTS]
    sem = pltpu.SemaphoreType.DMA
    far_away = pl.BlockSpec(memory_space=pltpu.HBM)
    near = pl.BlockSpec(memory_space=pltpu.VMEM)
    return pl.pallas_call(
        fetch_kernel,
        name="fetch",
        out_shape=(
            jax.ShapeDtypeStruct((NZ, NX, NG, span, SLICE, BLK), BF16),
            jax.ShapeDtypeStruct((1, PLANE * SLICE), I32),
            jax.ShapeDtypeStruct((count, width, points), BF16),
            jax.ShapeDtypeStruct((NZ * NX, span, BLK, BLK), F32),
        ),
        in_specs=[far_away] * 5,
        out_specs=(near,) * 4,
        scratch_shapes=[
            *part * 8,
            pltpu.VMEM((NZ, PLANE, span, SLICE, BLK), BF16),
            pltpu.VMEM((1, 128), I32),
            pltpu.VMEM((PLANE, 1, 128), I32),
            pltpu.VMEM((1, 128), I32),
            pltpu.SMEM((1, 128), I32),
            pltpu.VMEM(batch_blocks.shape, I32),
            pltpu.SMEM(block_live.shape, I32),
            pltpu.SMEM(live_functions.shape, I32),
            pltpu.VMEM((2 * count // NZ, points, width), BF16),
            sem((2,)), sem, sem, sem, sem((3,)), sem((2 * count // NZ,)), sem((16,)), sem((16,)),
            sem((2 * NZ,)), sem((2 * NZ,)),
        ],
        compiler_params=pltpu.CompilerParams(
            collective_id=0, has_side_effects=True, vmem_limit_bytes=16 * MIB
        ),
    )(
        *[
            pltpu.with_memory_space_constraint(a, pltpu.HBM)
            for a in (
                batch_blocks, block_live, live_functions,
                density.reshape(rows, span, NG, SLICE, BLK), basis_values,
            )
        ]
    )


def batch_kernel(blocks_ref, across_ref, weights_ref, region_ref, zeros_ref, site_ref, total):
    del zeros_ref
    slots, count = blocks_ref.shape
    half = slots * BLK // 2
    contract = (((1,), (1,)), ((), ()))

    def one(b):
        starts = [blocks_ref[k, b] for k in range(slots)]
        homes = [s & (NX * NZ - 1) for s in starts]
        across = across_ref[b]

        def tile(k, l):
            return region_ref[homes[k], :, starts[l] - starts[k]].reshape(BLK, BLK)

        wide = across.astype(F32)
        site = jnp.zeros((1, across.shape[1]), F32)
        for k in range(slots):
            tiles = jnp.concatenate([tile(k, l) for l in range(k, slots)], axis=1)
            product = jnp.dot(tiles, across[k * BLK :], preferred_element_type=F32)
            site += jnp.sum(product * wide[k * BLK : (k + 1) * BLK], axis=0, keepdims=True)
        site_ref[pl.ds(b, 1)] = site
        potential = weights_ref[pl.ds(b, 1)] * site / jnp.sqrt(1.0 + site * site)
        weighted = (potential * wide).astype(BF16)
        top = lax.dot_general(across[:half], weighted, contract, preferred_element_type=F32)
        low = lax.dot_general(
            across[half:], weighted[half:], contract, preferred_element_type=F32
        )
        return starts, homes, top, low

    def add(starts, homes, top, low):
        for k in range(slots):
            for l in range(k, slots):
                if k < slots // 2:
                    part = top[k * BLK : (k + 1) * BLK, l * BLK : (l + 1) * BLK]
                else:
                    i, j = k - slots // 2, l - slots // 2
                    part = low[i * BLK : (i + 1) * BLK, j * BLK : (j + 1) * BLK]
                total[homes[k], starts[l] - starts[k]] += part

    def some(i, carry):
        parts = [one(i * TOGETHER + j) for j in range(TOGETHER)]
        for part in parts:
            add(*part)
        return carry

    lax.fori_loop(0, count // TOGETHER, some, 0)


def batches(batch_blocks, weights, region, across, zeros):
    span = region.shape[3]
    near = pl.BlockSpec(memory_space=pltpu.VMEM)
    return pl.pallas_call(
        batch_kernel,
        name="batches",
        out_shape=(
            jax.ShapeDtypeStruct(weights.shape, F32),
            jax.ShapeDtypeStruct(zeros.shape, F32),
        ),
        in_specs=[pl.BlockSpec(memory_space=pltpu.SMEM)] + [near] * 4,
        out_specs=(near, near),
        input_output_aliases={4: 1},
        compiler_params=pltpu.CompilerParams(vmem_limit_bytes=12 * MIB),
    )(batch_blocks, across, weights, region.reshape(NZ * NX, NG, span, SLICE, BLK), zeros)


TOGETHER = 8
PIECES = (
    (4, 0, 3), (4, 3, 5), (3, 0, 3), (-3, 0, 3), (3, 3, 5), (-3, 3, 5), (2, 0, 3), (-2, 0, 3), (2, 3, 5), (-2, 3, 5), (1, 0, 3), (-1, 0, 3), (1, 3, 5), (-1, 3, 5), (0, 0, 3), (0, 3, 5),
)
HOPS = sum(1 if 0 < abs(off) < 4 else off // 2 for off, _, _ in PIECES)
OFFS = (4, 3, -3, 2, -2, 1, -1, 0)
AHEAD = 4


def give_kernel(
    live_ref, lanes_ref, total_ref, out_ref,
    got, send, s4, s3r, s3l, s2r, s2l, s1r, s1l, i3r, i3l, i2r, i2l, i1r, i1l, i0r, i0l,
    plane_send, plane_recv, ring_send, ring_recv,
):
    y, c, z, x = place()
    me = slot_of(y, c, x)
    right, left = (y, c, (z + 1) % NZ, x), (y, c, (z + NZ - 1) % NZ, x)
    rows, span = out_ref.shape[:2]
    depth = rows * SLICE
    half = depth // 2
    greet(y, c, z, x)

    def pack(n):
        off, low, high = PIECES[n]
        z_of = (z + off + NZ) % NZ
        for x2 in range(NX):
            for o in range(low, high):
                tile = total_ref[z_of * NX + x2, o].astype(BF16)
                send[OFFS.index(off), x2, :, o] = tile.reshape(NG, SLICE, BLK)

    def hand(n):
        off, low, high = PIECES[n]
        k = OFFS.index(off)
        piece = pl.ds(low, high - low)

        def one(i, carry):
            y2, c2, x2 = peer(i, y, c, x)
            remote(
                send.at[k, x2, y2 * NC + c2, piece], got.at[k, me, piece], plane_send.at[n],
                plane_recv.at[n], (y2, c2, z, x2),
            ).start()
            return carry

        lax.fori_loop(1, PLANE, one, 0)
        pltpu.make_async_copy(
            send.at[k, x, y * NC + c, piece], got.at[k, me, piece], plane_recv.at[n]
        ).start()

    lane = lax.broadcasted_iota(I32, lanes_ref.shape, 1) % SLICE
    first = lanes_ref[...]
    row_index = lax.broadcasted_iota(I32, (depth, PLANE * SLICE), 0)

    def partials(n):
        off, low, high = PIECES[n]
        k = OFFS.index(off)
        await_bytes(got.at[k, :, pl.ds(low, high - low)], plane_recv.at[n])
        m = ((z + off + NZ) % NZ) * NX + x
        wanted = lax.shift_right_logical(first + ((m - first) & (NX * NZ - 1)), 5)
        key = wanted * SLICE + lane
        chosen = jnp.where(row_index == key, 1.0, 0.0).astype(BF16)
        for o in range(low, high):
            block = got[k, :, o].reshape(PLANE * SLICE, BLK)
            yield o, jnp.dot(chosen, block, preferred_element_type=F32)

    hops = {}
    waited = set()

    def hop(n, src, dst, where):
        place_of = len(hops)
        copy = remote(src, dst, ring_send.at[place_of], ring_recv.at[place_of], where)
        copy.start()
        hops[n] = copy

    pack(0)
    await_greetings()
    hand(0)
    for n in range(1, AHEAD):
        pack(n)
        hand(n)
    mine = {3: s3r, -3: s3l, 2: s2r, -2: s2l, 1: s1r, -1: s1l}
    came = {3: i3r, -3: i3l, 2: i2r, -2: i2l, 1: i1r, -1: i1l, 0: i0r}
    goes = {3: i2r, -3: i2l, 2: i1r, -2: i1l, 1: i0r, -1: i0l}
    for n, (off, low, high) in enumerate(PIECES):
        if n >= 1 and n + AHEAD - 1 < len(PIECES):
            pack(n + AHEAD - 1)
            hand(n + AHEAD - 1)
        piece = pl.ds(low, high - low)
        for o, part in partials(n):
            if off == 4:
                s4[o] = part.astype(BF16)
                continue
            if o == low:
                sources = [(4 if off == -3 else off + step, step) for step in (1, -1) if off * step >= 0]
                for key in list(hops):
                    near = key[:2] in sources and key[2] < high and key[3] > low
                    if near and key not in waited:
                        hops[key].wait_recv()
                        waited.add(key)
            if off == 3:
                mine[off][o, :half] = (part[:half] + came[off][o].astype(F32)).astype(BF16)
                mine[off][o, half:] = part[half:].astype(BF16)
            elif off == -3:
                mine[off][o, :half] = part[:half].astype(BF16)
                mine[off][o, half:] = (part[half:] + came[off][o].astype(F32)).astype(BF16)
            elif off:
                mine[off][o] = (part + came[off][o].astype(F32)).astype(BF16)
            else:
                total = part + i0r[o].astype(F32) + i0l[o].astype(F32)
                for t in range(rows):
                    live = live_ref[o, t].astype(F32)
                    out_ref[t, o] = (total[t * SLICE : (t + 1) * SLICE] * live).astype(BF16)
        if off == 4:
            top, low_half = pl.ds(0, half), pl.ds(half, half)
            hop((4, 1, low, high), s4.at[piece, top], i3r.at[piece], right)
            hop((4, -1, low, high), s4.at[piece, low_half], i3l.at[piece], left)
        elif off:
            step = 1 if off > 0 else -1
            where = right if off > 0 else left
            hop((off, step, low, high), mine[off].at[piece], goes[off].at[piece], where)
    for copy in hops.values():
        copy.wait_send()
    others = pl.ds(1, PLANE - 1)
    for n, (off, low, high) in enumerate(PIECES):
        await_bytes(got.at[OFFS.index(off), others, pl.ds(low, high - low)], plane_send.at[n])


def give(block_live, lanes, total):
    span, rows = total.shape[1], block_live.shape[1]
    sem = pltpu.SemaphoreType.DMA
    whole = pltpu.VMEM((span, rows * SLICE, BLK), BF16)
    part = pltpu.VMEM((span, rows * SLICE // 2, BLK), BF16)
    near = pl.BlockSpec(memory_space=pltpu.VMEM)
    return pl.pallas_call(
        give_kernel,
        name="give",
        out_shape=jax.ShapeDtypeStruct((rows, span, SLICE, BLK), BF16),
        in_specs=[pl.BlockSpec(memory_space=pltpu.SMEM), near, near],
        out_specs=near,
        scratch_shapes=[
            pltpu.VMEM((NZ, PLANE, span, SLICE, BLK), BF16),
            pltpu.VMEM((NZ, NX, NG, span, SLICE, BLK), BF16),
            *[whole] * 7,
            part, part, *[whole] * 6,
            sem((len(PIECES),)), sem((len(PIECES),)), sem((HOPS,)), sem((HOPS,)),
        ],
        compiler_params=pltpu.CompilerParams(
            collective_id=1, has_side_effects=True, vmem_limit_bytes=24 * MIB
        ),
    )(block_live, lanes, total)


def per_device(basis_values, weights, density, block_live, batch_blocks, live_functions):
    batch_blocks, block_live = batch_blocks.T, block_live.T
    region, lanes, across, zeros = fetch(
        batch_blocks, block_live, live_functions, density, basis_values
    )
    site_density, total = batches(batch_blocks, weights, region, across, zeros)
    return site_density, give(block_live, lanes, total)


def solution(mesh):
    split = Mesh(mesh.devices.reshape(NY, NC, NZ, NX), AXES)
    placed = (
        P(AXES, None, None),
        P(AXES, None),
        P(MAT, None, None, None),
        P(MAT, None),
        P(AXES, None),
        P(AXES),
    )
    return jax.shard_map(
        per_device,
        mesh=split,
        in_specs=placed,
        out_specs=(P(AXES, None), P(MAT, None, GRP, None)),
        check_vma=False,
    )
```

```python
import jax
import jax.numpy as jnp
from jax import lax
from jax.experimental import pallas as pl
from jax.experimental.pallas import tpu as pltpu
from jax.sharding import Mesh
from jax.sharding import PartitionSpec as P

AXES = ("y", "c", "z", "x")
MAT = ("z", "x")
GRP = ("y", "c")
NX, NY, NZ, NC = 4, 4, 8, 2
NG = NY * NC
PLANE = NX * NG
BLK = 128
SLICE = BLK // NG
MESH = pl.DeviceIdType.MESH
MIB = 1 << 20
BF16, F32, I32 = jnp.bfloat16, jnp.float32, jnp.int32


def place():
    return tuple(lax.axis_index(a) for a in AXES)


def peer(i, y, c, x):
    row = lax.div(i, NX)
    return (
        lax.rem(y + lax.rem(row, NY), NY),
        lax.rem(c + lax.div(row, NY), NC),
        lax.rem(x + lax.rem(i, NX), NX),
    )


def slot_of(y, c, x):
    return x * NG + y * NC + c


def greet(y, c, z, x):
    barrier = pltpu.get_barrier_semaphore()

    def signal(i, carry):
        y2, c2, x2 = peer(i, y, c, x)
        pl.semaphore_signal(barrier, inc=1, device_id=(y2, c2, z, x2), device_id_type=MESH)
        return carry

    lax.fori_loop(1, PLANE, signal, 0, unroll=True)
    for step in (1, NZ - 1):
        pl.semaphore_signal(
            barrier, inc=1, device_id=(y, c, (z + step) % NZ, x), device_id_type=MESH
        )


def await_greetings():
    pl.semaphore_wait(pltpu.get_barrier_semaphore(), PLANE + 1)


def remote(src, dst, send_sem, recv_sem, where):
    return pltpu.make_async_remote_copy(
        src_ref=src,
        dst_ref=dst,
        send_sem=send_sem,
        recv_sem=recv_sem,
        device_id=where,
        device_id_type=MESH,
    )


def await_bytes(ref, sem):
    pltpu.make_async_copy(ref, ref, sem).wait()


PARTS = ((0, 3), (3, 5))


def fetch_kernel(
    blocks_hbm, live_hbm, functions_hbm, density_ref, values_ref,
    region_ref, lanes_ref, across_ref, total_ref,
    own_a, own_b, r1_a, r1_b, r2_a, r2_b, r3_a, r3_b, l1_a, l1_b, l2_a, l2_b, l3_a, l3_b,
    far_a, far_b, send, first, firsts, row, firsts_s, blocks_ref, live_ref,
    functions_ref, raw,
    load_sem, first_send, first_recv, table_sem, small_sem, value_sem, ring_send, ring_recv,
    plane_send, plane_recv,
):
    y, c, z, x = place()
    g = y * NC + c
    me = slot_of(y, c, x)
    right, left = (y, c, (z + 1) % NZ, x), (y, c, (z + NZ - 1) % NZ, x)
    small = [
        pltpu.make_async_copy(blocks_hbm, blocks_ref, small_sem.at[0]),
        pltpu.make_async_copy(live_hbm, live_ref, small_sem.at[1]),
        pltpu.make_async_copy(functions_hbm, functions_ref, small_sem.at[2]),
    ]
    for copy in small:
        copy.start()
    own, far = (own_a, own_b), (far_a, far_b)
    r1, r2, r3 = (r1_a, r1_b), (r2_a, r2_b), (r3_a, r3_b)
    l1, l2, l3 = (l1_a, l1_b), (l2_a, l2_b), (l3_a, l3_b)
    loads = [
        pltpu.make_async_copy(density_ref.at[:, pl.ds(low, high - low), g], part, load_sem.at[p])
        for p, ((low, high), part) in enumerate(zip(PARTS, own))
    ]
    for load in loads:
        load.start()
    greet(y, c, z, x)
    small[0].wait()
    first[...] = jnp.broadcast_to(jnp.min(blocks_ref[...], keepdims=True), first.shape)
    await_greetings()

    def tell(i, carry):
        y2, c2, x2 = peer(i, y, c, x)
        remote(first, firsts.at[me], first_send, first_recv, (y2, c2, z, x2)).start()
        return carry

    lax.fori_loop(1, PLANE, tell, 0, unroll=True)
    pltpu.make_async_copy(first, firsts.at[me], first_recv).start()

    small[1].wait()
    small[2].wait()
    for load in loads:
        load.wait()
    rows = own_a.shape[0]

    def mask(t, carry):
        for (low, high), part in zip(PARTS, own):
            for o in range(low, high):
                scale = live_ref[o, t].astype(F32) * (2.0 if o else 1.0)
                part[t, o - low] = part[t, o - low] * scale.astype(BF16)
        return carry

    lax.fori_loop(0, rows, mask, 0)

    hops = []

    def hop(src, dst, where):
        k = len(hops)
        copy = remote(src, dst, ring_send.at[k], ring_recv.at[k], where)
        copy.start()
        hops.append(copy)
        return copy

    half = rows // 2
    first_hops = [(hop(own[p], r1[p], right), hop(own[p], l1[p], left)) for p in range(2)]
    count = values_ref.shape[0]
    per = count // NZ

    def bring(b):
        slot = b % (2 * per)
        return pltpu.make_async_copy(values_ref.at[b], raw.at[slot], value_sem.at[slot])

    for b in range(per):
        bring(b).start()
    await_bytes(firsts, first_recv)
    lane = lax.broadcasted_iota(I32, (1, 128), 1)
    held = firsts[0]
    for d in range(1, PLANE):
        held = jnp.where(lane == d, firsts[d], held)
    row[...] = held
    table = pltpu.make_async_copy(row, firsts_s, table_sem)
    table.start()
    table.wait()

    def serve(k, p, source, z_of):
        m = z_of * NX + x
        low, high = PARTS[p]
        piece = pl.ds(low, high - low)

        def wanted(d):
            f = firsts_s[0, d]
            return lax.shift_right_logical(f + ((m - f) & (NX * NZ - 1)), 5)

        def one(i, carry):
            y2, c2, x2 = peer(i, y, c, x)
            send[k, i, low:high] = source[p][wanted(slot_of(y2, c2, x2))]
            remote(
                send.at[k, i, piece], region_ref.at[z_of, x, g, piece], plane_send.at[2 * k + p],
                plane_recv.at[2 * k + p], (y2, c2, z, x2),
            ).start()
            return carry

        lax.fori_loop(1, PLANE, one, 0)
        send[k, 0, low:high] = source[p][wanted(me)]
        pltpu.make_async_copy(
            send.at[k, 0, piece], region_ref.at[z_of, x, g, piece], plane_recv.at[2 * k + p]
        ).start()

    def prepare(k):
        for b in range(k * per, (k + 1) * per):
            if b + per < count:
                bring(b + per).start()
        for b in range(k * per, (k + 1) * per):
            bring(b).wait()
            across = raw[b % (2 * per)].T
            function_index = lax.broadcasted_iota(I32, across.shape, 0)
            across_ref[b] = jnp.where(
                function_index < functions_ref[b], across, jnp.zeros_like(across)
            )
        step = total_ref.shape[0] // NZ

        @pl.loop(k * step, (k + 1) * step)
        def _(m):
            total_ref[m] = jnp.zeros(total_ref.shape[1:], F32)

    serve(0, 0, own, z)
    serve(0, 1, own, z)
    prepare(0)
    came = first_hops
    for step, (rs, ls, rd, ld) in enumerate(((r1, l1, r2, l2), (r2, l2, r3, l3), (r3, l3, far, far)), 1):
        goes = []
        for p in range(2):
            for side in range(2):
                came[p][side].wait_recv()
                source, target, where = ((rs, rd, right), (ls, ld, left))[side]
                source, target = source[p], target[p]
                if step == 3:
                    rows_of = pl.ds(side * half, half)
                    source, target = source.at[rows_of], target.at[rows_of]
                goes.append(hop(source, target, where))
            serve(2 * step - 1, p, rs, (z + NZ - step) % NZ)
            serve(2 * step, p, ls, (z + step) % NZ)
        came = [goes[:2], goes[2:]]
        prepare(2 * step - 1)
        prepare(2 * step)
    for p in range(2):
        came[p][0].wait_recv()
        came[p][1].wait_recv()
        serve(7, p, far, (z + NZ // 2) % NZ)
    prepare(7)
    lane = lane // SLICE
    for chunk in range(PLANE * SLICE // 128):
        held = firsts[chunk * 8]
        for d in range(1, 8):
            held = jnp.where(lane == d, firsts[chunk * 8 + d], held)
        lanes_ref[:, chunk * 128 : (chunk + 1) * 128] = held
    for copy in hops:
        copy.wait_send()
    others = pl.ds(1, PLANE - 1)
    await_bytes(firsts.at[others], first_send)
    for k, off in enumerate((0, NZ - 1, 1, NZ - 2, 2, NZ - 3, 3, NZ // 2)):
        for p, (low, high) in enumerate(PARTS):
            piece = pl.ds(low, high - low)
            await_bytes(send.at[k, others, piece], plane_send.at[2 * k + p])
            arrived = region_ref.at[(z + off) % NZ, :, :, piece]
            await_bytes(arrived, plane_recv.at[2 * k + p])


def fetch(batch_blocks, block_live, live_functions, density, basis_values):
    rows, span = density.shape[:2]
    count, points, width = basis_values.shape
    part = [pltpu.VMEM((rows, high - low, SLICE, BLK), BF16) for low, high in PARTS]
    sem = pltpu.SemaphoreType.DMA
    far_away = pl.BlockSpec(memory_space=pltpu.HBM)
    near = pl.BlockSpec(memory_space=pltpu.VMEM)
    return pl.pallas_call(
        fetch_kernel,
        name="fetch",
        out_shape=(
            jax.ShapeDtypeStruct((NZ, NX, NG, span, SLICE, BLK), BF16),
            jax.ShapeDtypeStruct((1, PLANE * SLICE), I32),
            jax.ShapeDtypeStruct((count, width, points), BF16),
            jax.ShapeDtypeStruct((NZ * NX, span, BLK, BLK), F32),
        ),
        in_specs=[far_away] * 5,
        out_specs=(near,) * 4,
        scratch_shapes=[
            *part * 8,
            pltpu.VMEM((NZ, PLANE, span, SLICE, BLK), BF16),
            pltpu.VMEM((1, 128), I32),
            pltpu.VMEM((PLANE, 1, 128), I32),
            pltpu.VMEM((1, 128), I32),
            pltpu.SMEM((1, 128), I32),
            pltpu.VMEM(batch_blocks.shape, I32),
            pltpu.SMEM(block_live.shape, I32),
            pltpu.SMEM(live_functions.shape, I32),
            pltpu.VMEM((2 * count // NZ, points, width), BF16),
            sem((2,)), sem, sem, sem, sem((3,)), sem((2 * count // NZ,)), sem((16,)), sem((16,)),
            sem((2 * NZ,)), sem((2 * NZ,)),
        ],
        compiler_params=pltpu.CompilerParams(
            collective_id=0, has_side_effects=True, vmem_limit_bytes=16 * MIB
        ),
    )(
        *[
            pltpu.with_memory_space_constraint(a, pltpu.HBM)
            for a in (
                batch_blocks, block_live, live_functions,
                density.reshape(rows, span, NG, SLICE, BLK), basis_values,
            )
        ]
    )


def batch_kernel(blocks_ref, across_ref, weights_ref, region_ref, zeros_ref, site_ref, total):
    del zeros_ref
    slots, count = blocks_ref.shape
    half = slots * BLK // 2
    contract = (((1,), (1,)), ((), ()))

    def one(b):
        starts = [blocks_ref[k, b] for k in range(slots)]
        homes = [s & (NX * NZ - 1) for s in starts]
        across = across_ref[b]

        def tile(k, l):
            return region_ref[homes[k], :, starts[l] - starts[k]].reshape(BLK, BLK)

        wide = across.astype(F32)
        site = jnp.zeros((1, across.shape[1]), F32)
        for k in range(slots):
            tiles = jnp.concatenate([tile(k, l) for l in range(k, slots)], axis=1)
            product = jnp.dot(tiles, across[k * BLK :], preferred_element_type=F32)
            site += jnp.sum(product * wide[k * BLK : (k + 1) * BLK], axis=0, keepdims=True)
        site_ref[pl.ds(b, 1)] = site
        potential = weights_ref[pl.ds(b, 1)] * site / jnp.sqrt(1.0 + site * site)
        weighted = (potential * wide).astype(BF16)
        return starts, homes, across, weighted

    def add(starts, homes, across, weighted):
        top = lax.dot_general(across[:half], weighted, contract, preferred_element_type=F32)
        low = lax.dot_general(
            across[half:], weighted[half:], contract, preferred_element_type=F32
        )
        for k in range(slots):
            for l in range(k, slots):
                if k < slots // 2:
                    part = top[k * BLK : (k + 1) * BLK, l * BLK : (l + 1) * BLK]
                else:
                    i, j = k - slots // 2, l - slots // 2
                    part = low[i * BLK : (i + 1) * BLK, j * BLK : (j + 1) * BLK]
                total[homes[k], starts[l] - starts[k]] += part

    def some(i, carry):
        held = one(i * TOGETHER)
        for j in range(1, TOGETHER):
            later = one(i * TOGETHER + j)
            add(*held)
            held = later
        add(*held)
        return carry

    lax.fori_loop(0, count // TOGETHER, some, 0)


def batches(batch_blocks, weights, region, across, zeros):
    span = region.shape[3]
    near = pl.BlockSpec(memory_space=pltpu.VMEM)
    return pl.pallas_call(
        batch_kernel,
        name="batches",
        out_shape=(
            jax.ShapeDtypeStruct(weights.shape, F32),
            jax.ShapeDtypeStruct(zeros.shape, F32),
        ),
        in_specs=[pl.BlockSpec(memory_space=pltpu.SMEM)] + [near] * 4,
        out_specs=(near, near),
        input_output_aliases={4: 1},
        compiler_params=pltpu.CompilerParams(vmem_limit_bytes=12 * MIB),
    )(batch_blocks, across, weights, region.reshape(NZ * NX, NG, span, SLICE, BLK), zeros)


TOGETHER = 8
PIECES = (
    (4, 0, 3), (4, 3, 5), (3, 0, 3), (-3, 0, 3), (3, 3, 5), (-3, 3, 5), (2, 0, 3), (-2, 0, 3), (2, 3, 5), (-2, 3, 5), (1, 0, 3), (-1, 0, 3), (1, 3, 5), (-1, 3, 5), (0, 0, 3), (0, 3, 5),
)
HOPS = sum(1 if 0 < abs(off) < 4 else off // 2 for off, _, _ in PIECES)
OFFS = (4, 3, -3, 2, -2, 1, -1, 0)
AHEAD = 4


def give_kernel(
    live_ref, lanes_ref, total_ref, out_ref,
    got, send, s4, s3r, s3l, s2r, s2l, s1r, s1l, i3r, i3l, i2r, i2l, i1r, i1l, i0r, i0l,
    plane_send, plane_recv, ring_send, ring_recv,
):
    y, c, z, x = place()
    me = slot_of(y, c, x)
    right, left = (y, c, (z + 1) % NZ, x), (y, c, (z + NZ - 1) % NZ, x)
    rows, span = out_ref.shape[:2]
    depth = rows * SLICE
    half = depth // 2
    greet(y, c, z, x)

    def pack(n):
        off, low, high = PIECES[n]
        z_of = (z + off + NZ) % NZ
        for x2 in range(NX):
            for o in range(low, high):
                tile = total_ref[z_of * NX + x2, o].astype(BF16)
                send[OFFS.index(off), x2, :, o] = tile.reshape(NG, SLICE, BLK)

    def hand(n):
        off, low, high = PIECES[n]
        k = OFFS.index(off)
        piece = pl.ds(low, high - low)

        def one(i, carry):
            y2, c2, x2 = peer(i, y, c, x)
            remote(
                send.at[k, x2, y2 * NC + c2, piece], got.at[k, me, piece], plane_send.at[n],
                plane_recv.at[n], (y2, c2, z, x2),
            ).start()
            return carry

        lax.fori_loop(1, PLANE, one, 0)
        pltpu.make_async_copy(
            send.at[k, x, y * NC + c, piece], got.at[k, me, piece], plane_recv.at[n]
        ).start()

    lane = lax.broadcasted_iota(I32, lanes_ref.shape, 1) % SLICE
    first = lanes_ref[...]
    row_index = lax.broadcasted_iota(I32, (depth, PLANE * SLICE), 0)

    def partials(n):
        off, low, high = PIECES[n]
        k = OFFS.index(off)
        await_bytes(got.at[k, :, pl.ds(low, high - low)], plane_recv.at[n])
        m = ((z + off + NZ) % NZ) * NX + x
        wanted = lax.shift_right_logical(first + ((m - first) & (NX * NZ - 1)), 5)
        key = wanted * SLICE + lane
        chosen = jnp.where(row_index == key, 1.0, 0.0).astype(BF16)
        for o in range(low, high):
            block = got[k, :, o].reshape(PLANE * SLICE, BLK)
            yield o, jnp.dot(chosen, block, preferred_element_type=F32)

    hops = {}
    waited = set()

    def hop(n, src, dst, where):
        place_of = len(hops)
        copy = remote(src, dst, ring_send.at[place_of], ring_recv.at[place_of], where)
        copy.start()
        hops[n] = copy

    pack(0)
    await_greetings()
    hand(0)
    for n in range(1, AHEAD):
        pack(n)
        hand(n)
    mine = {3: s3r, -3: s3l, 2: s2r, -2: s2l, 1: s1r, -1: s1l}
    came = {3: i3r, -3: i3l, 2: i2r, -2: i2l, 1: i1r, -1: i1l, 0: i0r}
    goes = {3: i2r, -3: i2l, 2: i1r, -2: i1l, 1: i0r, -1: i0l}
    for n, (off, low, high) in enumerate(PIECES):
        if n >= 1 and n + AHEAD - 1 < len(PIECES):
            pack(n + AHEAD - 1)
            hand(n + AHEAD - 1)
        piece = pl.ds(low, high - low)
        for o, part in partials(n):
            if off == 4:
                s4[o] = part.astype(BF16)
                continue
            if o == low:
                sources = [(4 if off == -3 else off + step, step) for step in (1, -1) if off * step >= 0]
                for key in list(hops):
                    near = key[:2] in sources and key[2] < high and key[3] > low
                    if near and key not in waited:
                        hops[key].wait_recv()
                        waited.add(key)
            if off == 3:
                mine[off][o, :half] = (part[:half] + came[off][o].astype(F32)).astype(BF16)
                mine[off][o, half:] = part[half:].astype(BF16)
            elif off == -3:
                mine[off][o, :half] = part[:half].astype(BF16)
                mine[off][o, half:] = (part[half:] + came[off][o].astype(F32)).astype(BF16)
            elif off:
                mine[off][o] = (part + came[off][o].astype(F32)).astype(BF16)
            else:
                total = part + i0r[o].astype(F32) + i0l[o].astype(F32)
                for t in range(rows):
                    live = live_ref[o, t].astype(F32)
                    out_ref[t, o] = (total[t * SLICE : (t + 1) * SLICE] * live).astype(BF16)
        if off == 4:
            top, low_half = pl.ds(0, half), pl.ds(half, half)
            hop((4, 1, low, high), s4.at[piece, top], i3r.at[piece], right)
            hop((4, -1, low, high), s4.at[piece, low_half], i3l.at[piece], left)
        elif off:
            step = 1 if off > 0 else -1
            where = right if off > 0 else left
            hop((off, step, low, high), mine[off].at[piece], goes[off].at[piece], where)
    for copy in hops.values():
        copy.wait_send()
    others = pl.ds(1, PLANE - 1)
    for n, (off, low, high) in enumerate(PIECES):
        await_bytes(got.at[OFFS.index(off), others, pl.ds(low, high - low)], plane_send.at[n])


def give(block_live, lanes, total):
    span, rows = total.shape[1], block_live.shape[1]
    sem = pltpu.SemaphoreType.DMA
    whole = pltpu.VMEM((span, rows * SLICE, BLK), BF16)
    part = pltpu.VMEM((span, rows * SLICE // 2, BLK), BF16)
    near = pl.BlockSpec(memory_space=pltpu.VMEM)
    return pl.pallas_call(
        give_kernel,
        name="give",
        out_shape=jax.ShapeDtypeStruct((rows, span, SLICE, BLK), BF16),
        in_specs=[pl.BlockSpec(memory_space=pltpu.SMEM), near, near],
        out_specs=near,
        scratch_shapes=[
            pltpu.VMEM((NZ, PLANE, span, SLICE, BLK), BF16),
            pltpu.VMEM((NZ, NX, NG, span, SLICE, BLK), BF16),
            *[whole] * 7,
            part, part, *[whole] * 6,
            sem((len(PIECES),)), sem((len(PIECES),)), sem((HOPS,)), sem((HOPS,)),
        ],
        compiler_params=pltpu.CompilerParams(
            collective_id=1, has_side_effects=True, vmem_limit_bytes=24 * MIB
        ),
    )(block_live, lanes, total)


def per_device(basis_values, weights, density, block_live, batch_blocks, live_functions):
    batch_blocks, block_live = batch_blocks.T, block_live.T
    region, lanes, across, zeros = fetch(
        batch_blocks, block_live, live_functions, density, basis_values
    )
    site_density, total = batches(batch_blocks, weights, region, across, zeros)
    return site_density, give(block_live, lanes, total)


def solution(mesh):
    split = Mesh(mesh.devices.reshape(NY, NC, NZ, NX), AXES)
    placed = (
        P(AXES, None, None),
        P(AXES, None),
        P(MAT, None, None, None),
        P(MAT, None),
        P(AXES, None),
        P(AXES),
    )
    return jax.shard_map(
        per_device,
        mesh=split,
        in_specs=placed,
        out_specs=(P(AXES, None), P(MAT, None, GRP, None)),
        check_vma=False,
    )
```

```python
import jax
import jax.numpy as jnp
from jax import lax
from jax.experimental import pallas as pl
from jax.experimental.pallas import tpu as pltpu
from jax.sharding import Mesh
from jax.sharding import PartitionSpec as P

AXES = ("y", "c", "z", "x")
MAT = ("z", "x")
GRP = ("y", "c")
NX, NY, NZ, NC = 4, 4, 8, 2
NG = NY * NC
PLANE = NX * NG
BLK = 128
SLICE = BLK // NG
MESH = pl.DeviceIdType.MESH
MIB = 1 << 20
BF16, F32, I32 = jnp.bfloat16, jnp.float32, jnp.int32


def place():
    return tuple(lax.axis_index(a) for a in AXES)


def peer(i, y, c, x):
    row = lax.div(i, NX)
    return (
        lax.rem(y + lax.rem(row, NY), NY),
        lax.rem(c + lax.div(row, NY), NC),
        lax.rem(x + lax.rem(i, NX), NX),
    )


def slot_of(y, c, x):
    return x * NG + y * NC + c


def greet(y, c, z, x):
    barrier = pltpu.get_barrier_semaphore()

    def signal(i, carry):
        y2, c2, x2 = peer(i, y, c, x)
        pl.semaphore_signal(barrier, inc=1, device_id=(y2, c2, z, x2), device_id_type=MESH)
        return carry

    lax.fori_loop(1, PLANE, signal, 0, unroll=True)
    for step in (1, NZ - 1):
        pl.semaphore_signal(
            barrier, inc=1, device_id=(y, c, (z + step) % NZ, x), device_id_type=MESH
        )


def await_greetings():
    pl.semaphore_wait(pltpu.get_barrier_semaphore(), PLANE + 1)


def remote(src, dst, send_sem, recv_sem, where):
    return pltpu.make_async_remote_copy(
        src_ref=src,
        dst_ref=dst,
        send_sem=send_sem,
        recv_sem=recv_sem,
        device_id=where,
        device_id_type=MESH,
    )


def await_bytes(ref, sem):
    pltpu.make_async_copy(ref, ref, sem).wait()


PARTS = ((0, 3), (3, 5))


def fetch_kernel(
    blocks_hbm, live_hbm, functions_hbm, density_ref, values_ref,
    region_ref, lanes_ref, across_ref, total_ref,
    own_a, own_b, r1_a, r1_b, r2_a, r2_b, r3_a, r3_b, l1_a, l1_b, l2_a, l2_b, l3_a, l3_b,
    far_a, far_b, send, first, firsts, row, firsts_s, blocks_ref, live_ref,
    functions_ref, raw,
    load_sem, first_send, first_recv, table_sem, small_sem, value_sem, ring_send, ring_recv,
    plane_send, plane_recv,
):
    y, c, z, x = place()
    g = y * NC + c
    me = slot_of(y, c, x)
    right, left = (y, c, (z + 1) % NZ, x), (y, c, (z + NZ - 1) % NZ, x)
    small = [
        pltpu.make_async_copy(blocks_hbm, blocks_ref, small_sem.at[0]),
        pltpu.make_async_copy(live_hbm, live_ref, small_sem.at[1]),
        pltpu.make_async_copy(functions_hbm, functions_ref, small_sem.at[2]),
    ]
    for copy in small:
        copy.start()
    own, far = (own_a, own_b), (far_a, far_b)
    r1, r2, r3 = (r1_a, r1_b), (r2_a, r2_b), (r3_a, r3_b)
    l1, l2, l3 = (l1_a, l1_b), (l2_a, l2_b), (l3_a, l3_b)
    loads = [
        pltpu.make_async_copy(density_ref.at[:, pl.ds(low, high - low), g], part, load_sem.at[p])
        for p, ((low, high), part) in enumerate(zip(PARTS, own))
    ]
    for load in loads:
        load.start()
    greet(y, c, z, x)
    small[0].wait()
    first[...] = jnp.broadcast_to(jnp.min(blocks_ref[...], keepdims=True), first.shape)
    await_greetings()

    def tell(i, carry):
        y2, c2, x2 = peer(i, y, c, x)
        remote(first, firsts.at[me], first_send, first_recv, (y2, c2, z, x2)).start()
        return carry

    lax.fori_loop(1, PLANE, tell, 0, unroll=True)
    pltpu.make_async_copy(first, firsts.at[me], first_recv).start()

    small[1].wait()
    small[2].wait()
    for load in loads:
        load.wait()
    rows = own_a.shape[0]

    def mask(t, carry):
        for (low, high), part in zip(PARTS, own):
            for o in range(low, high):
                scale = live_ref[o, t].astype(F32) * (2.0 if o else 1.0)
                part[t, o - low] = part[t, o - low] * scale.astype(BF16)
        return carry

    lax.fori_loop(0, rows, mask, 0)

    hops = []

    def hop(src, dst, where):
        k = len(hops)
        copy = remote(src, dst, ring_send.at[k], ring_recv.at[k], where)
        copy.start()
        hops.append(copy)
        return copy

    half = rows // 2
    first_hops = [(hop(own[p], r1[p], right), hop(own[p], l1[p], left)) for p in range(2)]
    count = values_ref.shape[0]
    per = count // NZ

    def bring(b):
        slot = b % (2 * per)
        return pltpu.make_async_copy(values_ref.at[b], raw.at[slot], value_sem.at[slot])

    for b in range(per):
        bring(b).start()
    await_bytes(firsts, first_recv)
    lane = lax.broadcasted_iota(I32, (1, 128), 1)
    held = firsts[0]
    for d in range(1, PLANE):
        held = jnp.where(lane == d, firsts[d], held)
    row[...] = held
    table = pltpu.make_async_copy(row, firsts_s, table_sem)
    table.start()
    table.wait()

    def serve(k, p, source, z_of):
        m = z_of * NX + x
        low, high = PARTS[p]
        piece = pl.ds(low, high - low)

        def wanted(d):
            f = firsts_s[0, d]
            return lax.shift_right_logical(f + ((m - f) & (NX * NZ - 1)), 5)

        def one(i, carry):
            y2, c2, x2 = peer(i, y, c, x)
            send[k, i, low:high] = source[p][wanted(slot_of(y2, c2, x2))]
            remote(
                send.at[k, i, piece], region_ref.at[z_of, x, g, piece], plane_send.at[2 * k + p],
                plane_recv.at[2 * k + p], (y2, c2, z, x2),
            ).start()
            return carry

        lax.fori_loop(1, PLANE, one, 0)
        send[k, 0, low:high] = source[p][wanted(me)]
        pltpu.make_async_copy(
            send.at[k, 0, piece], region_ref.at[z_of, x, g, piece], plane_recv.at[2 * k + p]
        ).start()

    def prepare(k):
        for b in range(k * per, (k + 1) * per):
            if b + per < count:
                bring(b + per).start()
        for b in range(k * per, (k + 1) * per):
            bring(b).wait()
            across = raw[b % (2 * per)].T
            function_index = lax.broadcasted_iota(I32, across.shape, 0)
            across_ref[b] = jnp.where(
                function_index < functions_ref[b], across, jnp.zeros_like(across)
            )
        step = total_ref.shape[0] // NZ

        @pl.loop(k * step, (k + 1) * step)
        def _(m):
            total_ref[m] = jnp.zeros(total_ref.shape[1:], F32)

    serve(0, 0, own, z)
    serve(0, 1, own, z)
    prepare(0)
    came = first_hops
    for step, (rs, ls, rd, ld) in enumerate(((r1, l1, r2, l2), (r2, l2, r3, l3), (r3, l3, far, far)), 1):
        goes = []
        for p in range(2):
            for side in range(2):
                came[p][side].wait_recv()
                source, target, where = ((rs, rd, right), (ls, ld, left))[side]
                source, target = source[p], target[p]
                if step == 3:
                    rows_of = pl.ds(side * half, half)
                    source, target = source.at[rows_of], target.at[rows_of]
                goes.append(hop(source, target, where))
            serve(2 * step - 1, p, rs, (z + NZ - step) % NZ)
            serve(2 * step, p, ls, (z + step) % NZ)
        came = [goes[:2], goes[2:]]
        prepare(2 * step - 1)
        prepare(2 * step)
    for p in range(2):
        came[p][0].wait_recv()
        came[p][1].wait_recv()
        serve(7, p, far, (z + NZ // 2) % NZ)
    prepare(7)
    lane = lane // SLICE
    for chunk in range(PLANE * SLICE // 128):
        held = firsts[chunk * 8]
        for d in range(1, 8):
            held = jnp.where(lane == d, firsts[chunk * 8 + d], held)
        lanes_ref[:, chunk * 128 : (chunk + 1) * 128] = held
    for copy in hops:
        copy.wait_send()
    others = pl.ds(1, PLANE - 1)
    await_bytes(firsts.at[others], first_send)
    for k, off in enumerate((0, NZ - 1, 1, NZ - 2, 2, NZ - 3, 3, NZ // 2)):
        for p, (low, high) in enumerate(PARTS):
            piece = pl.ds(low, high - low)
            await_bytes(send.at[k, others, piece], plane_send.at[2 * k + p])
            arrived = region_ref.at[(z + off) % NZ, :, :, piece]
            await_bytes(arrived, plane_recv.at[2 * k + p])


def fetch(batch_blocks, block_live, live_functions, density, basis_values):
    rows, span = density.shape[:2]
    count, points, width = basis_values.shape
    part = [pltpu.VMEM((rows, high - low, SLICE, BLK), BF16) for low, high in PARTS]
    sem = pltpu.SemaphoreType.DMA
    far_away = pl.BlockSpec(memory_space=pltpu.HBM)
    near = pl.BlockSpec(memory_space=pltpu.VMEM)
    return pl.pallas_call(
        fetch_kernel,
        name="fetch",
        out_shape=(
            jax.ShapeDtypeStruct((NZ, NX, NG, span, SLICE, BLK), BF16),
            jax.ShapeDtypeStruct((1, PLANE * SLICE), I32),
            jax.ShapeDtypeStruct((count, width, points), BF16),
            jax.ShapeDtypeStruct((NZ * NX, span, BLK, BLK), F32),
        ),
        in_specs=[far_away] * 5,
        out_specs=(near,) * 4,
        scratch_shapes=[
            *part * 8,
            pltpu.VMEM((NZ, PLANE, span, SLICE, BLK), BF16),
            pltpu.VMEM((1, 128), I32),
            pltpu.VMEM((PLANE, 1, 128), I32),
            pltpu.VMEM((1, 128), I32),
            pltpu.SMEM((1, 128), I32),
            pltpu.VMEM(batch_blocks.shape, I32),
            pltpu.SMEM(block_live.shape, I32),
            pltpu.SMEM(live_functions.shape, I32),
            pltpu.VMEM((2 * count // NZ, points, width), BF16),
            sem((2,)), sem, sem, sem, sem((3,)), sem((2 * count // NZ,)), sem((16,)), sem((16,)),
            sem((2 * NZ,)), sem((2 * NZ,)),
        ],
        compiler_params=pltpu.CompilerParams(
            collective_id=0, has_side_effects=True, vmem_limit_bytes=16 * MIB
        ),
    )(
        *[
            pltpu.with_memory_space_constraint(a, pltpu.HBM)
            for a in (
                batch_blocks, block_live, live_functions,
                density.reshape(rows, span, NG, SLICE, BLK), basis_values,
            )
        ]
    )


def batch_kernel(blocks_ref, across_ref, weights_ref, region_ref, zeros_ref, site_ref, total):
    del zeros_ref
    slots, count = blocks_ref.shape
    half = slots * BLK // 2
    contract = (((1,), (1,)), ((), ()))

    def one(b):
        starts = [blocks_ref[k, b] for k in range(slots)]
        homes = [s & (NX * NZ - 1) for s in starts]
        across = across_ref[b]

        def tile(k, l):
            return region_ref[homes[k], :, starts[l] - starts[k]].reshape(BLK, BLK)

        wide = across.astype(F32)
        none = jnp.zeros((BLK, BLK), BF16)

        def rows(low, high):
            return jnp.concatenate(
                [
                    jnp.concatenate(
                        [tile(k, l) if l >= k else none for l in range(low, slots)], axis=1
                    )
                    for k in range(low, high)
                ],
                axis=0,
            )

        first = jnp.dot(rows(0, slots // 2), across, preferred_element_type=F32)
        last = jnp.dot(rows(slots // 2, slots), across[half:], preferred_element_type=F32)
        site = jnp.sum(first * wide[:half], axis=0, keepdims=True)
        site += jnp.sum(last * wide[half:], axis=0, keepdims=True)
        site_ref[pl.ds(b, 1)] = site
        potential = weights_ref[pl.ds(b, 1)] * site / jnp.sqrt(1.0 + site * site)
        weighted = (potential * wide).astype(BF16)
        return starts, homes, across, weighted

    def add(starts, homes, across, weighted):
        top = lax.dot_general(across[:half], weighted, contract, preferred_element_type=F32)
        low = lax.dot_general(
            across[half:], weighted[half:], contract, preferred_element_type=F32
        )
        for k in range(slots):
            for l in range(k, slots):
                if k < slots // 2:
                    part = top[k * BLK : (k + 1) * BLK, l * BLK : (l + 1) * BLK]
                else:
                    i, j = k - slots // 2, l - slots // 2
                    part = low[i * BLK : (i + 1) * BLK, j * BLK : (j + 1) * BLK]
                total[homes[k], starts[l] - starts[k]] += part

    def some(i, carry):
        held = one(i * TOGETHER)
        for j in range(1, TOGETHER):
            later = one(i * TOGETHER + j)
            add(*held)
            held = later
        add(*held)
        return carry

    lax.fori_loop(0, count // TOGETHER, some, 0)


def batches(batch_blocks, weights, region, across, zeros):
    span = region.shape[3]
    near = pl.BlockSpec(memory_space=pltpu.VMEM)
    return pl.pallas_call(
        batch_kernel,
        name="batches",
        out_shape=(
            jax.ShapeDtypeStruct(weights.shape, F32),
            jax.ShapeDtypeStruct(zeros.shape, F32),
        ),
        in_specs=[pl.BlockSpec(memory_space=pltpu.SMEM)] + [near] * 4,
        out_specs=(near, near),
        input_output_aliases={4: 1},
        compiler_params=pltpu.CompilerParams(vmem_limit_bytes=12 * MIB),
    )(batch_blocks, across, weights, region.reshape(NZ * NX, NG, span, SLICE, BLK), zeros)


TOGETHER = 16
PIECES = (
    (4, 0, 3), (4, 3, 5), (3, 0, 3), (-3, 0, 3), (3, 3, 5), (-3, 3, 5), (2, 0, 3), (-2, 0, 3), (2, 3, 5), (-2, 3, 5), (1, 0, 3), (-1, 0, 3), (1, 3, 5), (-1, 3, 5), (0, 0, 3), (0, 3, 5),
)
HOPS = sum(1 if 0 < abs(off) < 4 else off // 2 for off, _, _ in PIECES)
OFFS = (4, 3, -3, 2, -2, 1, -1, 0)
AHEAD = 4


def give_kernel(
    live_ref, lanes_ref, total_ref, out_ref,
    got, send, s4, s3r, s3l, s2r, s2l, s1r, s1l, i3r, i3l, i2r, i2l, i1r, i1l, i0r, i0l,
    plane_send, plane_recv, ring_send, ring_recv,
):
    y, c, z, x = place()
    me = slot_of(y, c, x)
    right, left = (y, c, (z + 1) % NZ, x), (y, c, (z + NZ - 1) % NZ, x)
    rows, span = out_ref.shape[:2]
    depth = rows * SLICE
    half = depth // 2
    greet(y, c, z, x)

    def pack(n):
        off, low, high = PIECES[n]
        z_of = (z + off + NZ) % NZ
        for x2 in range(NX):
            for o in range(low, high):
                tile = total_ref[z_of * NX + x2, o].astype(BF16)
                send[OFFS.index(off), x2, :, o] = tile.reshape(NG, SLICE, BLK)

    def hand(n):
        off, low, high = PIECES[n]
        k = OFFS.index(off)
        piece = pl.ds(low, high - low)

        def one(i, carry):
            y2, c2, x2 = peer(i, y, c, x)
            remote(
                send.at[k, x2, y2 * NC + c2, piece], got.at[k, me, piece], plane_send.at[n],
                plane_recv.at[n], (y2, c2, z, x2),
            ).start()
            return carry

        lax.fori_loop(1, PLANE, one, 0)
        pltpu.make_async_copy(
            send.at[k, x, y * NC + c, piece], got.at[k, me, piece], plane_recv.at[n]
        ).start()

    lane = lax.broadcasted_iota(I32, lanes_ref.shape, 1) % SLICE
    first = lanes_ref[...]
    row_index = lax.broadcasted_iota(I32, (depth, PLANE * SLICE), 0)

    def partials(n):
        off, low, high = PIECES[n]
        k = OFFS.index(off)
        await_bytes(got.at[k, :, pl.ds(low, high - low)], plane_recv.at[n])
        m = ((z + off + NZ) % NZ) * NX + x
        wanted = lax.shift_right_logical(first + ((m - first) & (NX * NZ - 1)), 5)
        key = wanted * SLICE + lane
        chosen = jnp.where(row_index == key, 1.0, 0.0).astype(BF16)
        for o in range(low, high):
            block = got[k, :, o].reshape(PLANE * SLICE, BLK)
            yield o, jnp.dot(chosen, block, preferred_element_type=F32)

    hops = {}
    waited = set()

    def hop(n, src, dst, where):
        place_of = len(hops)
        copy = remote(src, dst, ring_send.at[place_of], ring_recv.at[place_of], where)
        copy.start()
        hops[n] = copy

    pack(0)
    await_greetings()
    hand(0)
    for n in range(1, AHEAD):
        pack(n)
        hand(n)
    mine = {3: s3r, -3: s3l, 2: s2r, -2: s2l, 1: s1r, -1: s1l}
    came = {3: i3r, -3: i3l, 2: i2r, -2: i2l, 1: i1r, -1: i1l, 0: i0r}
    goes = {3: i2r, -3: i2l, 2: i1r, -2: i1l, 1: i0r, -1: i0l}
    for n, (off, low, high) in enumerate(PIECES):
        if n >= 1 and n + AHEAD - 1 < len(PIECES):
            pack(n + AHEAD - 1)
            hand(n + AHEAD - 1)
        piece = pl.ds(low, high - low)
        for o, part in partials(n):
            if off == 4:
                s4[o] = part.astype(BF16)
                continue
            if o == low:
                sources = [(4 if off == -3 else off + step, step) for step in (1, -1) if off * step >= 0]
                for key in list(hops):
                    near = key[:2] in sources and key[2] < high and key[3] > low
                    if near and key not in waited:
                        hops[key].wait_recv()
                        waited.add(key)
            if off == 3:
                mine[off][o, :half] = (part[:half] + came[off][o].astype(F32)).astype(BF16)
                mine[off][o, half:] = part[half:].astype(BF16)
            elif off == -3:
                mine[off][o, :half] = part[:half].astype(BF16)
                mine[off][o, half:] = (part[half:] + came[off][o].astype(F32)).astype(BF16)
            elif off:
                mine[off][o] = (part + came[off][o].astype(F32)).astype(BF16)
            else:
                total = part + i0r[o].astype(F32) + i0l[o].astype(F32)
                for t in range(rows):
                    live = live_ref[o, t].astype(F32)
                    out_ref[t, o] = (total[t * SLICE : (t + 1) * SLICE] * live).astype(BF16)
        if off == 4:
            top, low_half = pl.ds(0, half), pl.ds(half, half)
            hop((4, 1, low, high), s4.at[piece, top], i3r.at[piece], right)
            hop((4, -1, low, high), s4.at[piece, low_half], i3l.at[piece], left)
        elif off:
            step = 1 if off > 0 else -1
            where = right if off > 0 else left
            hop((off, step, low, high), mine[off].at[piece], goes[off].at[piece], where)
    for copy in hops.values():
        copy.wait_send()
    others = pl.ds(1, PLANE - 1)
    for n, (off, low, high) in enumerate(PIECES):
        await_bytes(got.at[OFFS.index(off), others, pl.ds(low, high - low)], plane_send.at[n])


def give(block_live, lanes, total):
    span, rows = total.shape[1], block_live.shape[1]
    sem = pltpu.SemaphoreType.DMA
    whole = pltpu.VMEM((span, rows * SLICE, BLK), BF16)
    part = pltpu.VMEM((span, rows * SLICE // 2, BLK), BF16)
    near = pl.BlockSpec(memory_space=pltpu.VMEM)
    return pl.pallas_call(
        give_kernel,
        name="give",
        out_shape=jax.ShapeDtypeStruct((rows, span, SLICE, BLK), BF16),
        in_specs=[pl.BlockSpec(memory_space=pltpu.SMEM), near, near],
        out_specs=near,
        scratch_shapes=[
            pltpu.VMEM((NZ, PLANE, span, SLICE, BLK), BF16),
            pltpu.VMEM((NZ, NX, NG, span, SLICE, BLK), BF16),
            *[whole] * 7,
            part, part, *[whole] * 6,
            sem((len(PIECES),)), sem((len(PIECES),)), sem((HOPS,)), sem((HOPS,)),
        ],
        compiler_params=pltpu.CompilerParams(
            collective_id=1, has_side_effects=True, vmem_limit_bytes=24 * MIB
        ),
    )(block_live, lanes, total)


def per_device(basis_values, weights, density, block_live, batch_blocks, live_functions):
    batch_blocks, block_live = batch_blocks.T, block_live.T
    region, lanes, across, zeros = fetch(
        batch_blocks, block_live, live_functions, density, basis_values
    )
    site_density, total = batches(batch_blocks, weights, region, across, zeros)
    return site_density, give(block_live, lanes, total)


def solution(mesh):
    split = Mesh(mesh.devices.reshape(NY, NC, NZ, NX), AXES)
    placed = (
        P(AXES, None, None),
        P(AXES, None),
        P(MAT, None, None, None),
        P(MAT, None),
        P(AXES, None),
        P(AXES),
    )
    return jax.shard_map(
        per_device,
        mesh=split,
        in_specs=placed,
        out_specs=(P(AXES, None), P(MAT, None, GRP, None)),
        check_vma=False,
    )
```
